128 devices in a mesh: section: 4 (over x_lo, core), seq: 8 (over x_hi, z), tp: 4 (over y).
Axes of the slice: x: 4 (x_hi: 2, x_lo: 2; x = x_hi * 2 + x_lo), y: 4, z: 4, core: 2. Of those that a mesh axis runs over, the one named last changes fastest.
Arguments:
- streams: float32 [4, 4, 1024, 1280], P('section', None, 'seq'), may hold values from -6 to 6
- head_streams: float32 [4, 1024, 1280], P(None, 'seq'), may hold values from -6 to 6
- gains: float32 [4, 2, 1280], P('section'), may hold values from 0.1 to 1.9
- w_qkv: bfloat16 [4, 1280, 3, 1280], P('section', None, None, 'tp'), may hold values from -40 to 40
- w_out: bfloat16 [4, 1280, 1280], P('section', None, 'tp'), may hold values from -0.15625 to 0.15625
- w_up: bfloat16 [4, 1280, 5120], P('section', None, 'tp'), may hold values from -0.15625 to 0.15625
- w_down: bfloat16 [4, 1280, 5120], P('section', None, 'tp'), may hold values from -0.078125 to 0.078125
Outputs:
- recon: float32 [4, 4, 1024, 1280], P('section', None, 'seq')
- grad_qkv: bfloat16 [4, 1280, 3, 1280], P('section', 'seq', None, 'tp')
- grad_out: bfloat16 [4, 1280, 1280], P('section', 'seq', 'tp')
- grad_up: bfloat16 [4, 1280, 5120], P('section', 'seq', 'tp')
- grad_down: bfloat16 [4, 1280, 5120], P('section', 'seq', 'tp')
The draws below stay inside these ranges and needn't reach their ends.
All inputs are finite; a program needn't handle non-finite values.
Results may differ from the reference program's by a relative error of at most 0.028.
Values may be sent and summed in bfloat16 or wider, within the bound.
A program may use at most 128 MiB of HBM per device.

```python
import jax
import jax.numpy as jnp
from jax import lax

D = 1280
HEADS = 20
HEAD_DIM = 64
FF = 5120
TOK_DEV = 128
SECTIONS = 4
TOKENS = 1024
N_SEQ = 8


def draw_w_qkv(key, part):
    scale = D ** (-0.5)
    base = jnp.clip(jax.random.normal(key, (SECTIONS, D, 3, D), jnp.float32), -6.0, 6.0)
    factor = jnp.where(jnp.arange(3) < 2, 1.4, 1.0)
    weight = base * scale * factor[None, None, :, None]
    return weight.astype(jnp.bfloat16)


def levels(rng, extent, shards, smallest, largest):
    def one(dim, blocks):
        steps = jax.random.uniform(jax.random.fold_in(jax.random.fold_in(rng, 6), dim), (blocks,), jnp.float32, smallest / len(shards), largest / len(shards))
        return jnp.repeat(jnp.exp(steps), extent[dim] // blocks).reshape((-1,) + (1,) * (len(extent) - dim - 1))

    loudness = one(*shards[0])
    for cut in shards[1:]:
        loudness = loudness * one(*cut)
    return loudness


def scatter_about(rng, extent, width, most, pieces=(), kind=jnp.bfloat16):
    drawn = jax.random.normal(rng, extent, jnp.float32) * width
    if len(pieces) > 0:
        drawn = levels(rng, extent, pieces, -0.22, 0.18) * drawn
    return jnp.clip(drawn, min=-most, max=most).astype(kind)


def setup_inputs(seed: int = 0) -> dict:
    seeds = jax.random.split(jax.random.key(seed), 8)
    return {
        "streams": scatter_about(seeds[0], (SECTIONS, 4, TOKENS, D), 1.0, 6.0, ((0, 4), (2, 8)), jnp.float32),
        "head_streams": scatter_about(seeds[1], (4, TOKENS, D), 1.0, 6.0, ((1, 8),), jnp.float32),
        "gains": jnp.clip(1.0 + 0.18 * jax.random.normal(seeds[2], (SECTIONS, 2, D), jnp.float32), 0.1, 1.9),
        "w_qkv": draw_w_qkv(jax.random.fold_in(seeds[7], 71), 0),
        "w_out": scatter_about(seeds[4], (SECTIONS, D, D), D ** -0.5, 0.15625, ((0, 4), (2, 4))),
        "w_up": scatter_about(seeds[5], (SECTIONS, D, FF), D ** -0.5, 0.15625, ((0, 4), (2, 4))),
        "w_down": scatter_about(seeds[6], (SECTIONS, D, FF), FF ** -0.5, 0.078125, ((0, 4), (2, 4))),
    }


def layer_norm(values, gain):
    centre = values - lax.optimization_barrier(jnp.mean(values, -1, keepdims=True))
    inv_std = lax.rsqrt(lax.optimization_barrier(jnp.mean(centre * centre, -1, keepdims=True)) + 1e-06)
    unit_vals = centre * inv_std
    return (unit_vals * gain, unit_vals, inv_std)

def norm_back(grad, gain, unit_vals, inv_std):
    scaled = grad * gain
    return inv_std * (scaled - lax.optimization_barrier(jnp.mean(scaled, -1, keepdims=True)) - unit_vals * lax.optimization_barrier(jnp.mean(scaled * unit_vals, -1, keepdims=True)))

def gelu_tanh(values):
    return jax.nn.gelu(values, approximate=True)

def attend_head(operands):
    query, keys, values, grad_mixed = operands
    scores = jnp.dot(query, keys.T, preferred_element_type=jnp.float32) * 0.125
    top = lax.optimization_barrier(jnp.max(scores, -1, keepdims=True))
    lse = top + jnp.log(lax.optimization_barrier(jnp.sum(jnp.exp(scores - top), -1, keepdims=True)))
    probs = jnp.exp(scores - lse)
    probs_low = probs.astype(jnp.bfloat16)
    mixed = jnp.dot(probs_low, values, preferred_element_type=jnp.float32).astype(jnp.bfloat16)
    grad_probs = jnp.dot(grad_mixed, values.T, preferred_element_type=jnp.float32)
    delta = lax.optimization_barrier(jnp.sum(probs * grad_probs, -1, keepdims=True))
    grad_scores = (probs * (grad_probs - delta)).astype(jnp.bfloat16)
    grad_query = (0.125 * jnp.dot(grad_scores, keys, preferred_element_type=jnp.float32)).astype(jnp.bfloat16)
    grad_keys = (0.125 * jnp.dot(grad_scores.T, query, preferred_element_type=jnp.float32)).astype(jnp.bfloat16)
    grad_values = jnp.dot(probs_low.T, grad_mixed, preferred_element_type=jnp.float32).astype(jnp.bfloat16)
    return (mixed, grad_query, grad_keys, grad_values)

def split_heads(values):
    return values.reshape(TOKENS, HEADS, HEAD_DIM).transpose(1, 0, 2)

def join_heads(values):
    return values.transpose(1, 0, 2).reshape(TOKENS, D)

def block(inputs, gain_pair, w_qkv, w_out, w_up, w_down):
    upper, lower, grad_upper, grad_lower = (inputs[0], inputs[1], inputs[2], inputs[3])
    normed_up, unit_up, inv_up = layer_norm(upper, gain_pair[1])
    normed_low = normed_up.astype(jnp.bfloat16)
    hidden_pre = jnp.dot(normed_low, w_up, preferred_element_type=jnp.float32)
    hidden = gelu_tanh(hidden_pre).astype(jnp.bfloat16)
    mlp_out = jnp.dot(hidden, w_down.T, preferred_element_type=jnp.float32)
    lower_in = lower - mlp_out
    normed_att, unit_att, inv_att = layer_norm(lower_in, gain_pair[0])
    att_low = normed_att.astype(jnp.bfloat16)
    w_flat = w_qkv.reshape(D, 3 * D)
    projected = jnp.dot(att_low, w_flat, preferred_element_type=jnp.float32).astype(jnp.bfloat16).reshape(TOKENS, 3, D)
    grad_lower_low = grad_lower.astype(jnp.bfloat16)
    grad_hidden = jnp.dot(grad_lower_low, w_down, preferred_element_type=jnp.float32)
    unused, pull = jax.vjp(gelu_tanh, hidden_pre)
    grad_pre = pull(grad_hidden)[0].astype(jnp.bfloat16)
    grad_normed = jnp.dot(grad_pre, w_up.T, preferred_element_type=jnp.float32)
    upper_total = grad_upper + norm_back(grad_normed, gain_pair[1], unit_up, inv_up)
    total_low = upper_total.astype(jnp.bfloat16)
    grad_mixed = jnp.dot(total_low, w_out, preferred_element_type=jnp.float32).astype(jnp.bfloat16)
    mixed, grad_query, grad_keys, grad_values = lax.map(attend_head, (split_heads(projected[:, 0]), split_heads(projected[:, 1]), split_heads(projected[:, 2]), split_heads(grad_mixed)))
    mixed = join_heads(mixed)
    att_out = jnp.dot(mixed, w_out.T, preferred_element_type=jnp.float32)
    upper_in = upper - att_out
    grad_proj = jnp.stack([join_heads(grad_query), join_heads(grad_keys), join_heads(grad_values)], 1).reshape(TOKENS, 3 * D)
    grad_att = jnp.dot(grad_proj, w_flat.T, preferred_element_type=jnp.float32)
    grad_lower_in = grad_lower + norm_back(grad_att, gain_pair[0], unit_att, inv_att)
    recon = jnp.stack([upper_in, lower_in, upper_total, grad_lower_in])
    factors = ((att_low, grad_proj), (total_low, mixed), (normed_low, grad_pre), (grad_lower_low, hidden))
    return (recon, factors)

def shard_terms(left, right):
    left_rows = left.astype(jnp.float32).reshape(N_SEQ, TOK_DEV, -1)
    right_rows = right.astype(jnp.float32).reshape(N_SEQ, TOK_DEV, -1)
    return jnp.einsum('ntd,nte->nde', left_rows, right_rows, precision=lax.Precision.HIGHEST)

def reference(streams, head_streams, gains, w_qkv, w_out, w_up, w_down):
    first = [block(streams[section], gains[section], w_qkv[section], w_out[section], w_up[section], w_down[section]) for section in range(SECTIONS)]
    recon_list = []
    grad_lists = [[], [], [], []]
    for section in range(SECTIONS):
        inputs = first[section + 1][0] if section + 1 < SECTIONS else head_streams
        recon, factors = block(inputs, gains[section], w_qkv[section], w_out[section], w_up[section], w_down[section])
        recon_list.append(recon)
        for index in range(4):
            totals = shard_terms(*first[section][1][index]) + shard_terms(*factors[index])
            part = lax.optimization_barrier(totals.astype(jnp.bfloat16))
            grad_lists[index].append(lax.optimization_barrier(jnp.sum(part.astype(jnp.float32), 0)).astype(jnp.bfloat16))
    grad_qkv = jnp.stack(grad_lists[0]).reshape(SECTIONS, D, 3, D)
    grad_out = jnp.stack(grad_lists[1])
    grad_up = jnp.stack(grad_lists[2])
    grad_down = jnp.stack(grad_lists[3])
    return (jnp.stack(recon_list), grad_qkv, grad_out, grad_up, grad_down)
```

```python
import math

import jax
import jax.numpy as jnp
from jax import lax
from jax.experimental import pallas as pl
from jax.experimental.pallas import tpu as pltpu
from jax.sharding import PartitionSpec as P

MESH = pl.DeviceIdType.MESH
BF16 = jnp.bfloat16
F32 = jnp.float32
HEAD_DIM = 64
PAIR = 2 * HEAD_DIM
N_TP = 4
N_Z = 4
N_SEQ = 8
N_SEC = 4
NU, GL, AL, TL = 0, 1, 2, 3
NN = (((1,), (0,)), ((), ()))
NT = (((1,), (1,)), ((), ()))
TN = (((0,), (0,)), ((), ()))


def dot(a, b, dims):
    return lax.dot_general(a, b, dims, preferred_element_type=F32)


def loop(count, size, body):
    def step(i, carry):
        body(pl.multiple_of(i * size, size))
        return carry

    lax.fori_loop(0, count, step, 0)


def unit_of(values):
    centre = values - jnp.mean(values, -1, keepdims=True)
    inv_std = lax.rsqrt(jnp.mean(centre * centre, -1, keepdims=True) + 1e-06)
    return centre * inv_std, inv_std


def norm_back(grad, gain, values):
    unit, inv_std = unit_of(values)
    scaled = grad * gain
    return inv_std * (
        scaled
        - jnp.mean(scaled, -1, keepdims=True)
        - unit * jnp.mean(scaled * unit, -1, keepdims=True)
    )


GELU_C = math.sqrt(2.0 / math.pi)


def gelu(x):
    return 0.5 * x * (1.0 + jnp.tanh(GELU_C * (x + 0.044715 * (x * x * x))))


def gelu_slope(x):
    t = jnp.tanh(GELU_C * (x + 0.044715 * (x * x * x)))
    return 0.5 * (1.0 + t) + 0.5 * x * (1.0 - t * t) * (GELU_C * (1.0 + 0.134145 * (x * x)))


class Sender:
    def __init__(self, send_sem, recv_sem):
        self.send_sem, self.recv_sem = send_sem, recv_sem
        self.all = []

    def start(self, src, dst, device):
        k = len(self.all)
        copy = pltpu.make_async_remote_copy(
            src_ref=src,
            dst_ref=dst,
            send_sem=self.send_sem.at[k],
            recv_sem=self.recv_sem.at[k],
            device_id=device,
            device_id_type=MESH,
        )
        copy.start()
        self.all.append(copy)
        return copy


def received(copies):
    for copy in copies:
        copy.wait_recv()


def kernel(sizes, *refs):
    rows, width, hid, att, cut_mlp, cut_att = sizes
    (streams_h, head_h, gains_h, wkv_h, wqo_h, wup_h, wdn_h) = refs[:7]
    (recon_h, gatt_h, gmlp_h) = refs[7:10]
    (
        xs, hd, gains, wkv, wqo, wup, wdn,
        rx, sx, fl, gp, hidden, dkvf, dqf, mxf,
        snd, rr, ag, kvb, dks, dkr, pre, qd, scores, pd,
        gmlp, gatt, ra_m, rz_m, rb_m, rw_m, ra_a, rz_a, rb_a, rw_a, om, oa,
        load_sem, out_sem, send_sem, recv_sem,
    ) = refs[10:]
    sec = lax.axis_index("section")
    seq = lax.axis_index("seq")
    tp = lax.axis_index("tp")
    x_hi, z = seq // N_Z, lax.rem(seq, N_Z)
    quarter = rows // N_TP
    chunk = width // N_SEQ
    half = width // 2
    mine = pl.ds(pl.multiple_of(tp * quarter, quarter), quarter)

    def tp_dev(d):
        return {"tp": lax.rem(tp + d, N_TP)}

    def seq_dev(d):
        return {"seq": lax.rem(x_hi + d // N_Z, 2) * N_Z + lax.rem(z + d % N_Z, N_Z)}

    def seq_back(d):
        return {"seq": lax.rem(x_hi + d // N_Z, 2) * N_Z + lax.rem(z + N_Z - d % N_Z, N_Z)}

    def sec_dev(by, d):
        return {"section": lax.rem(sec + by, N_SEC), "tp": lax.rem(tp + d, N_TP)}

    barrier = pltpu.get_barrier_semaphore()
    for d in range(1, N_TP):
        pl.semaphore_signal(barrier, inc=1, device_id=tp_dev(d), device_id_type=MESH)
    for d in range(1, N_SEQ):
        pl.semaphore_signal(barrier, inc=1, device_id=seq_dev(d), device_id_type=MESH)
    for d in range(N_TP):
        pl.semaphore_signal(barrier, inc=1, device_id=sec_dev(1, d), device_id_type=MESH)

    loads = []
    for k, (src, dst) in enumerate(
        ((streams_h, xs), (gains_h, gains), (wup_h, wup), (wdn_h, wdn), (wkv_h, wkv), (wqo_h, wqo), (head_h, hd))
    ):
        copy = pltpu.make_async_copy(src, dst, load_sem.at[k])
        copy.start()
        loads.append(copy)
    sender = Sender(send_sem, recv_sem)

    lane = lax.broadcasted_iota(jnp.int32, (rows, PAIR), 1)
    lane_all = lax.rem(lax.broadcasted_iota(jnp.int32, (rows, att), 1), PAIR)

    def peer_rows(d):
        return pl.ds(pl.multiple_of(lax.rem(tp + d, N_TP) * quarter, quarter), quarter)

    def scatter(t, k):
        return [
            sender.start(snd.at[t, k, peer_rows(d), :], rr.at[t, k, d - 1], tp_dev(d))
            for d in range(1, N_TP)
        ]

    def summed(t, k, copies):
        received(copies)
        total = snd[t, k, mine, :].astype(F32)
        for d in range(N_TP - 1):
            total = total + rr[t, k, d].astype(F32)
        return total

    def spread(slot, value):
        ag[slot, mine, :] = value.astype(BF16)
        return [
            sender.start(ag.at[slot, mine, :], ag.at[slot, mine, :], tp_dev(d)) for d in range(1, N_TP)
        ]

    def send_section(slot, value):
        sx[slot] = value.astype(BF16)
        return [
            sender.start(sx.at[slot], rx.at[slot * 3, mine, :], sec_dev(N_SEC - 1, d))
            for d in range(N_TP)
        ]

    def mlp_forward(t, x):
        gain = gains[1:2, :]

        def norm(r):
            unit, _ = unit_of(x[0, pl.ds(r, 32), :])
            fl[NU, pl.ds(t * rows + r, 32), :] = (unit * gain).astype(BF16)

        loop(rows // 32, 32, norm)

    def mlp_hidden(t):
        def up(c):
            out = dot(fl[NU, pl.ds(t * rows, rows), :], wup[:, pl.ds(c, 256)], NN)
            pre[:, pl.ds(c, 256)] = out
            hidden[pl.ds(t * rows, rows), pl.ds(c, 256)] = gelu(out).astype(BF16)

        loop(hid // 256, 256, up)

    def mlp_down(t):
        def down(c):
            snd[t, 0, :, pl.ds(c, 256)] = dot(
                hidden[pl.ds(t * rows, rows), :], wdn[pl.ds(c, 256), :], NT
            ).astype(BF16)

        loop(width // 256, 256, down)

    def mlp_back(t, x):
        def low(r):
            fl[GL, pl.ds(t * rows + r, 32), :] = x[3, pl.ds(r, 32), :].astype(BF16)

        loop(rows // 32, 32, low)

        def back(c):
            grad = dot(fl[GL, pl.ds(t * rows, rows), :], wdn[:, pl.ds(c, 256)], NN)
            gp[pl.ds(t * rows, rows), pl.ds(c, 256)] = (
                grad * gelu_slope(pre[:, pl.ds(c, 256)])
            ).astype(BF16)

        loop(hid // 256, 256, back)

        def out(c):
            snd[t, 1, :, pl.ds(c, 256)] = dot(
                gp[pl.ds(t * rows, rows), :], wup[pl.ds(c, 256), :], NT
            ).astype(BF16)

        loop(width // 256, 256, out)
        return scatter(t, 1)

    def attention_in(t, x, slot):
        gain = gains[0:1, :]

        def low(r):
            value = x[1, pl.ds(r, 32), :] - ag[slot, pl.ds(r, 32), :].astype(F32)
            x[1, pl.ds(r, 32), :] = value
            if t == 0:
                rx_low[pl.ds(r, 32), :] = value.astype(BF16)
            unit, _ = unit_of(value)
            fl[AL, pl.ds(t * rows + r, 32), :] = (unit * gain).astype(BF16)

        rx_low = snd.at[0, 0]
        loop(rows // 32, 32, low)
        kvb[t, 0] = dot(fl[AL, pl.ds(t * rows, rows), :], wkv[...], NN).astype(BF16)
        copies = [
            sender.start(kvb.at[t, 0], kvb.at[t, d], seq_dev(d)) for d in range(1, N_SEQ)
        ]
        query = dot(fl[AL, pl.ds(t * rows, rows), :], wqo[...], NN).astype(BF16).astype(F32) * 0.125
        qd[pl.ds(0, rows), :] = jnp.where(lane_all < HEAD_DIM, query, 0.0).astype(BF16)
        return copies

    def grads_in(t, x, slot):
        gain = gains[1:2, :]

        def total(r):
            grad = ag[slot, pl.ds(r, 32), :].astype(F32)
            value = x[2, pl.ds(r, 32), :] + norm_back(grad, gain, x[0, pl.ds(r, 32), :])
            x[2, pl.ds(r, 32), :] = value
            fl[TL, pl.ds(t * rows + r, 32), :] = value.astype(BF16)

        loop(rows // 32, 32, total)
        grad = dot(fl[TL, pl.ds(t * rows, rows), :], wqo[...], NN)
        qd[pl.ds(rows, rows), :] = jnp.where(lane_all >= HEAD_DIM, grad, 0.0).astype(BF16)

    def attend(t):
        tokens = N_SEQ * rows

        def head(c):
            lanes = pl.ds(c, PAIR)
            kv = kvb[t, :, :, lanes].reshape(tokens, PAIR)
            both = qd[:, lanes]
            scores[...] = dot(kv, both, NT)
            logits = scores[:, :rows]
            weight = jnp.exp(logits - jnp.max(logits, 0, keepdims=True))
            probs = weight * (1.0 / jnp.sum(weight, 0, keepdims=True))
            grad_probs = scores[:, rows:]
            delta = jnp.sum(probs * grad_probs, 0, keepdims=True)
            pd[:, rows:] = probs.astype(BF16)
            pd[:, :rows] = (probs * (grad_probs - delta)).astype(BF16)
            dks[t, :, :, lanes] = dot(pd[...], both, NN).astype(BF16).reshape(N_SEQ, rows, PAIR)
            mixed = dot(pd[...], kv, TN)
            dqf[pl.ds(t * rows, rows), lanes] = jnp.where(lane < HEAD_DIM, mixed[:rows] * 0.125, 0.0).astype(BF16)
            mxf[pl.ds(t * rows, rows), lanes] = jnp.where(lane >= HEAD_DIM, mixed[rows:], 0.0).astype(BF16)

        loop(att // PAIR, PAIR, head)
        return [
            sender.start(dks.at[t, d], dkr.at[t, d - 1], seq_back(d)) for d in range(1, N_SEQ)
        ]

    def attention_out(t):
        def out(c):
            snd[t, 2, :, pl.ds(c, 256)] = dot(
                mxf[pl.ds(t * rows, rows), :], wqo[pl.ds(c, 256), :], NT
            ).astype(BF16)

        loop(width // 256, 256, out)
        return scatter(t, 2)

    def attention_back(t, copies):
        received(copies)

        def add(r):
            total = dks[t, 0, pl.ds(r, 32), :].astype(F32)
            for d in range(N_SEQ - 1):
                total = total + dkr[t, d, pl.ds(r, 32), :].astype(F32)
            dkvf[pl.ds(t * rows + r, 32), :] = total.astype(BF16)

        loop(rows // 32, 32, add)

        def out(c):
            snd[t, 3, :, pl.ds(c, 256)] = (
                dot(dkvf[pl.ds(t * rows, rows), :], wkv[pl.ds(c, 256), :], NT)
                + dot(dqf[pl.ds(t * rows, rows), :], wqo[pl.ds(c, 256), :], NT)
            ).astype(BF16)

        loop(width // 256, 256, out)
        return scatter(t, 3)

    def grad_rows(by_x, by_z):
        index = lax.rem(x_hi + by_x, 2) * N_Z + lax.rem(z + by_z, N_Z)
        return pl.ds(pl.multiple_of(index * chunk, 32), chunk)

    def reduce_first(g, cut, ra, rb):
        other = pl.ds(pl.multiple_of((1 - x_hi) * half, 32), half)
        cols_a, cols_b = pl.ds(0, cut), pl.ds(cut, g.shape[1] - cut)
        first = [sender.start(g.at[other, cols_a], ra, seq_dev(N_Z))]
        second = []
        for d in range(1, N_Z):
            for k in range(2):
                second.append(sender.start(g.at[grad_rows(k, d), cols_b], rb.at[d - 1, k], seq_dev(d)))
        return first, second

    def reduce_second(g, cut, ra, rb, rz, rw, copies):
        first, second = copies
        cols_a, cols_b = pl.ds(0, cut), pl.ds(cut, g.shape[1] - cut)
        base = x_hi * half
        received(first)

        def add_a(r):
            here = pl.ds(pl.multiple_of(base + r, 32), 32)
            g[here, cols_a] = (g[here, cols_a].astype(F32) + ra[pl.ds(r, 32), :].astype(F32)).astype(BF16)

        loop(half // 32, 32, add_a)
        out = [
            sender.start(g.at[grad_rows(0, d), cols_a], rz.at[d - 1], seq_dev(d)) for d in range(1, N_Z)
        ]
        received(second)
        for k in (1, 0):
            start = (lax.rem(x_hi + k, 2) * N_Z + z) * chunk

            def add_b(r):
                here = pl.ds(pl.multiple_of(start + r, 32), 32)
                total = g[here, cols_b].astype(F32)
                for d in range(N_Z - 1):
                    total = total + rb[d, k, pl.ds(r, 32), :].astype(F32)
                g[here, cols_b] = total.astype(BF16)

            loop(chunk // 32, 32, add_b)
            if k == 1:
                out.append(sender.start(g.at[grad_rows(1, 0), cols_b], rw, seq_dev(N_Z)))
        return out

    def reduce_last(g, cut, rz, rw, out, dst, copies, sem):
        cols_a, cols_b = pl.ds(0, cut), pl.ds(cut, g.shape[1] - cut)
        received(copies)
        start = seq * chunk

        def add(r):
            here = pl.ds(pl.multiple_of(start + r, 32), 32)
            total = g[here, cols_a].astype(F32)
            for d in range(N_Z - 1):
                total = total + rz[d, pl.ds(r, 32), :].astype(F32)
            out[pl.ds(r, 32), cols_a] = total.astype(BF16)
            out[pl.ds(r, 32), cols_b] = (
                g[here, cols_b].astype(F32) + rw[pl.ds(r, 32), :].astype(F32)
            ).astype(BF16)

        loop(chunk // 32, 32, add)
        copy = pltpu.make_async_copy(out, dst, sem)
        copy.start()
        return copy

    def grads_mlp():
        def tile(c):
            gmlp[pl.ds(c, 256), pl.ds(0, hid)] = dot(fl[NU, :, pl.ds(c, 256)], gp[...], TN).astype(BF16)
            gmlp[pl.ds(c, 256), pl.ds(hid, hid)] = dot(fl[GL, :, pl.ds(c, 256)], hidden[...], TN).astype(BF16)

        loop(width // 256, 256, tile)
        return reduce_first(gmlp, cut_mlp, ra_m, rb_m)

    def grads_att():
        def tile(c):
            left = fl[AL, :, pl.ds(c, 256)]
            gatt[pl.ds(c, 256), pl.ds(0, att)] = dot(left, dkvf[...], TN).astype(BF16)
            gatt[pl.ds(c, 256), pl.ds(att, att)] = (
                dot(left, dqf[...], TN) + dot(fl[TL, :, pl.ds(c, 256)], mxf[...], TN)
            ).astype(BF16)

        loop(width // 256, 256, tile)
        return reduce_first(gatt, cut_att, ra_a, rb_a)

    loads[0].wait()
    loads[1].wait()
    mlp_forward(0, xs)
    loads[2].wait()
    mlp_hidden(0)
    loads[3].wait()
    mlp_down(0)
    pl.semaphore_wait(barrier, N_TP - 1 + N_SEQ - 1 + N_TP)
    c_mlp = scatter(0, 0)
    c_grad = mlp_back(0, xs)
    c_mlp = spread(0, summed(0, 0, c_mlp))
    c_grad = spread(1, summed(0, 1, c_grad))
    received(c_mlp)
    loads[4].wait()
    loads[5].wait()
    for copy in sender.all[:3]:
        copy.wait_send()
    c_kv = attention_in(0, xs, 0)
    c_low = sender.start(snd.at[0, 0], rx.at[1], sec_dev(N_SEC - 1, 0))
    received(c_grad)
    grads_in(0, xs, 1)
    c_total = sender.start(fl.at[TL, pl.ds(0, rows), :], rx.at[2], sec_dev(N_SEC - 1, 0))
    received(c_kv)
    c_dkv = attend(0)
    c_att = attention_out(0)
    c_up = send_section(0, xs[0, mine, :] - summed(0, 2, c_att))

    is_last = sec == N_SEC - 1
    loads[6].wait()

    def choose(k):
        def one(r):
            hd[k, pl.ds(r, 32), :] = jnp.where(
                is_last, hd[k, pl.ds(r, 32), :], rx[k, pl.ds(r, 32), :].astype(F32)
            )

        loop(rows // 32, 32, one)

    outs = []

    def emit(k):
        copy = pltpu.make_async_copy(hd.at[k], recon_h.at[k], out_sem.at[k])
        copy.start()
        outs.append(copy)

    slope = gains[0:1, :]
    c_att = attention_back(0, c_dkv)
    received(c_up)
    choose(0)
    mlp_forward(1, hd)
    mlp_hidden(1)
    mlp_down(1)
    c_mlp = scatter(1, 0)
    grad = summed(0, 3, c_att)
    c_gl = send_section(1, xs[3, mine, :] + norm_back(grad, slope, xs[1, mine, :]))
    c_mlp = spread(2, summed(1, 0, c_mlp))
    received([c_low])
    choose(1)
    received(c_mlp)
    c_kv = attention_in(1, hd, 2)
    emit(1)
    received(c_gl)
    choose(3)
    c_grad = mlp_back(1, hd)
    c_gm = grads_mlp()
    c_grad = spread(3, summed(1, 1, c_grad))
    received([c_total])
    choose(2)
    received(c_grad)
    grads_in(1, hd, 3)
    emit(2)
    received(c_kv)
    c_dkv = attend(1)
    c_att = attention_out(1)
    c_up = spread(4, summed(1, 2, c_att))
    c_att = attention_back(1, c_dkv)
    c_ga = grads_att()
    c_gl = spread(5, summed(1, 3, c_att))
    c_gm = reduce_second(gmlp, cut_mlp, ra_m, rb_m, rz_m, rw_m, c_gm)
    received(c_up)

    def upper(r):
        here = pl.ds(r, 32)
        value = hd[0, here, :]
        pre[here, :] = value - ag[4, here, :].astype(F32)

    loop(rows // 32, 32, upper)
    copy = pltpu.make_async_copy(pre, recon_h.at[0], out_sem.at[0])
    copy.start()
    outs.append(copy)
    received(c_gl)

    def lower(r):
        here = pl.ds(r, 32)
        hd[3, here, :] = hd[3, here, :] + norm_back(
            ag[5, here, :].astype(F32), slope, xs_low(here)
        )

    def xs_low(here):
        return hd[1, here, :]

    loop(rows // 32, 32, lower)
    emit(3)
    c_ga = reduce_second(gatt, cut_att, ra_a, rb_a, rz_a, rw_a, c_ga)
    outs.append(reduce_last(gmlp, cut_mlp, rz_m, rw_m, om, gmlp_h, c_gm, out_sem.at[4]))
    outs.append(reduce_last(gatt, cut_att, rz_a, rw_a, oa, gatt_h, c_ga, out_sem.at[5]))
    for copy in sender.all[3:]:
        copy.wait_send()
    for copy in outs:
        copy.wait()


N_COPIES = 104


def per_device(streams, head_streams, gains, w_qkv, w_out, w_up, w_down):
    rows, width = streams.shape[2], streams.shape[3]
    hid = w_up.shape[2]
    local = w_out.shape[2]
    att = 2 * local
    heads = local // HEAD_DIM
    chunk = width // N_SEQ
    half = width // 2
    cut_mlp = 1536
    cut_att = 768
    parts = w_qkv[0].reshape(width, 3, heads, HEAD_DIM)
    w_o = w_out[0].reshape(width, heads, HEAD_DIM)
    wkv = jnp.stack([parts[:, 1], parts[:, 2]], 2).reshape(width, att)
    wqo = jnp.stack([parts[:, 0], w_o], 2).reshape(width, att)
    sizes = (rows, width, hid, att, cut_mlp, cut_att)
    quarter = rows // N_TP
    rest_m, rest_a = 2 * hid - cut_mlp, 2 * att - cut_att
    vm = pltpu.VMEM
    scratch = [
        vm((4, rows, width), F32), vm((4, rows, width), F32), vm((2, width), F32),
        vm((width, att), BF16), vm((width, att), BF16), vm((width, hid), BF16), vm((width, hid), BF16),
        vm((4, rows, width), BF16), vm((2, quarter, width), BF16),
        vm((4, 2 * rows, width), BF16), vm((2 * rows, hid), BF16), vm((2 * rows, hid), BF16),
        vm((2 * rows, att), BF16), vm((2 * rows, att), BF16), vm((2 * rows, att), BF16),
        vm((2, 4, rows, width), BF16), vm((2, 4, N_TP - 1, quarter, width), BF16), vm((6, rows, width), BF16),
        vm((2, N_SEQ, rows, att), BF16), vm((2, N_SEQ, rows, att), BF16), vm((2, N_SEQ - 1, rows, att), BF16),
        vm((rows, hid), F32), vm((2 * rows, att), BF16),
        vm((N_SEQ * rows, 2 * rows), F32), vm((N_SEQ * rows, 2 * rows), BF16),
        vm((width, 2 * hid), BF16), vm((width, 2 * att), BF16),
        vm((half, cut_mlp), BF16), vm((N_Z - 1, chunk, cut_mlp), BF16),
        vm((N_Z - 1, 2, chunk, rest_m), BF16), vm((chunk, rest_m), BF16),
        vm((half, cut_att), BF16), vm((N_Z - 1, chunk, cut_att), BF16),
        vm((N_Z - 1, 2, chunk, rest_a), BF16), vm((chunk, rest_a), BF16),
        vm((chunk, 2 * hid), BF16), vm((chunk, 2 * att), BF16),
        pltpu.SemaphoreType.DMA((7,)), pltpu.SemaphoreType.DMA((6,)),
        pltpu.SemaphoreType.DMA((N_COPIES,)), pltpu.SemaphoreType.DMA((N_COPIES,)),
    ]
    any_spec = pl.BlockSpec(memory_space=pl.ANY)
    recon, gatt, gmlp = pl.pallas_call(
        lambda *refs: kernel(sizes, *refs),
        out_shape=(
            jax.ShapeDtypeStruct((4, rows, width), F32),
            jax.ShapeDtypeStruct((chunk, 2 * att), BF16),
            jax.ShapeDtypeStruct((chunk, 2 * hid), BF16),
        ),
        in_specs=[any_spec] * 7,
        out_specs=(any_spec,) * 3,
        scratch_shapes=scratch,
        compiler_params=pltpu.CompilerParams(
            collective_id=0, has_side_effects=True, vmem_limit_bytes=67043328
        ),
        name="window",
    )(streams[0], head_streams, gains[0], wkv, wqo, w_up[0], w_down[0])
    pairs = gatt.reshape(chunk, 2, heads, 2, HEAD_DIM)
    grad_qkv = jnp.stack([pairs[:, 1, :, 0], pairs[:, 0, :, 0], pairs[:, 0, :, 1]], 1).reshape(chunk, 3, local)
    grad_out = pairs[:, 1, :, 1].reshape(chunk, local)
    return (recon[None], grad_qkv[None], grad_out[None], gmlp[None, :, :hid], gmlp[None, :, hid:])


def solution(mesh):
    return jax.shard_map(
        per_device,
        mesh=mesh,
        in_specs=(
            P("section", None, "seq", None),
            P(None, "seq", None),
            P("section", None, None),
            P("section", None, None, "tp"),
            P("section", None, "tp"),
            P("section", None, "tp"),
            P("section", None, "tp"),
        ),
        out_specs=(
            P("section", None, "seq", None),
            P("section", "seq", None, "tp"),
            P("section", "seq", "tp"),
            P("section", "seq", "tp"),
            P("section", "seq", "tp"),
        ),
        check_vma=False,
    )
```

```python
import math

import jax
import jax.numpy as jnp
from jax import lax
from jax.experimental import pallas as pl
from jax.experimental.pallas import tpu as pltpu
from jax.sharding import PartitionSpec as P

MESH = pl.DeviceIdType.MESH
BF16 = jnp.bfloat16
F32 = jnp.float32
HEAD_DIM = 64
PAIR = 2 * HEAD_DIM
N_TP = 4
N_Z = 4
N_SEQ = 8
N_SEC = 4
KV_X_FIRST = 2
DKV_X_FIRST = 3
NU, GL, AL, TL = 0, 1, 2, 3
NN = (((1,), (0,)), ((), ()))
NT = (((1,), (1,)), ((), ()))
TN = (((0,), (0,)), ((), ()))


def dot(a, b, dims):
    return lax.dot_general(a, b, dims, preferred_element_type=F32)


def loop(count, size, body):
    def step(i, carry):
        body(pl.multiple_of(i * size, size))
        return carry

    lax.fori_loop(0, count, step, 0)


def unit_of(values):
    centre = values - jnp.mean(values, -1, keepdims=True)
    inv_std = lax.rsqrt(jnp.mean(centre * centre, -1, keepdims=True) + 1e-06)
    return centre * inv_std, inv_std


def norm_back(grad, gain, values):
    unit, inv_std = unit_of(values)
    scaled = grad * gain
    return inv_std * (
        scaled
        - jnp.mean(scaled, -1, keepdims=True)
        - unit * jnp.mean(scaled * unit, -1, keepdims=True)
    )


GELU_C = math.sqrt(2.0 / math.pi)


def gelu(x):
    return 0.5 * x * (1.0 + jnp.tanh(GELU_C * (x + 0.044715 * (x * x * x))))


def gelu_slope(x):
    t = jnp.tanh(GELU_C * (x + 0.044715 * (x * x * x)))
    return 0.5 * (1.0 + t) + 0.5 * x * (1.0 - t * t) * (GELU_C * (1.0 + 0.134145 * (x * x)))


class Sender:
    def __init__(self, send_sem, recv_sem):
        self.send_sem, self.recv_sem = send_sem, recv_sem
        self.all = []

    def start(self, src, dst, device):
        k = len(self.all)
        copy = pltpu.make_async_remote_copy(
            src_ref=src,
            dst_ref=dst,
            send_sem=self.send_sem.at[k],
            recv_sem=self.recv_sem.at[k],
            device_id=device,
            device_id_type=MESH,
        )
        copy.start()
        self.all.append(copy)
        return copy


def received(copies):
    for copy in copies:
        copy.wait_recv()


def kernel(sizes, *refs):
    rows, width, hid, att, cut_mlp, cut_att = sizes
    (streams_h, head_h, gains_h, wqkv_h, wout_h, wup_h, wdn_h) = refs[:7]
    (recon_h, gqkv_h, gout_h, gup_h, gdn_h) = refs[7:12]
    (
        xs, hd, gains, wkv, wqo, wup, wdn,
        rx, sx, fl, gp, hidden, dkvf, dqf, mxf,
        snd, rr, ag, kvb, dks, dax, daz, dbz, dbx, pre, qd, scores, pd,
        gmlp, gatt, ra_m, rz_m, rb_m, rw_m, ra_a, rz_a, rb_a, rw_a, om, oqkv, oout,
        load_sem, out_sem, send_sem, recv_sem,
    ) = refs[12:]
    heads = att // PAIR
    sec = lax.axis_index("section")
    seq = lax.axis_index("seq")
    tp = lax.axis_index("tp")
    x_hi, z = seq // N_Z, lax.rem(seq, N_Z)
    quarter = rows // N_TP
    chunk = width // N_SEQ
    half = width // 2
    mine = pl.ds(pl.multiple_of(tp * quarter, quarter), quarter)

    def tp_dev(d):
        return {"tp": lax.rem(tp + d, N_TP)}

    def seq_dev(d):
        return {"seq": lax.rem(x_hi + d // N_Z, 2) * N_Z + lax.rem(z + d % N_Z, N_Z)}

    def seq_back(d):
        return {"seq": lax.rem(x_hi + d // N_Z, 2) * N_Z + lax.rem(z + N_Z - d % N_Z, N_Z)}

    def sec_dev(by, d):
        return {"section": lax.rem(sec + by, N_SEC), "tp": lax.rem(tp + d, N_TP)}

    barrier = pltpu.get_barrier_semaphore()
    for d in range(1, N_TP):
        pl.semaphore_signal(barrier, inc=1, device_id=tp_dev(d), device_id_type=MESH)
    for d in range(1, N_SEQ):
        pl.semaphore_signal(barrier, inc=1, device_id=seq_dev(d), device_id_type=MESH)
    for d in range(N_TP):
        pl.semaphore_signal(barrier, inc=1, device_id=sec_dev(1, d), device_id_type=MESH)

    loads = []
    for k, (src, dst) in enumerate(
        (
            (streams_h, xs), (gains_h, gains), (wup_h, wup), (wdn_h, wdn),
            (wqkv_h.at[1], wkv.at[:, 0]), (wqkv_h.at[2], wkv.at[:, 1]),
            (wqkv_h.at[0], wqo.at[:, 0]), (wout_h, wqo.at[:, 1]), (head_h, hd),
        )
    ):
        copy = pltpu.make_async_copy(src, dst, load_sem.at[k])
        copy.start()
        loads.append(copy)
    sender = Sender(send_sem, recv_sem)

    lane = lax.broadcasted_iota(jnp.int32, (rows, PAIR), 1)
    lane_all = lax.rem(lax.broadcasted_iota(jnp.int32, (rows, att), 1), PAIR)

    def peer_rows(d):
        return pl.ds(pl.multiple_of(lax.rem(tp + d, N_TP) * quarter, quarter), quarter)

    def scatter(t, k):
        return [
            sender.start(snd.at[t, k, peer_rows(d), :], rr.at[t, k, d - 1], tp_dev(d))
            for d in range(1, N_TP)
        ]

    def summed(t, k, copies):
        received(copies)
        total = snd[t, k, mine, :].astype(F32)
        for d in range(N_TP - 1):
            total = total + rr[t, k, d].astype(F32)
        return total

    def spread(slot, value):
        ag[slot, mine, :] = value.astype(BF16)
        return [
            sender.start(ag.at[slot, mine, :], ag.at[slot, mine, :], tp_dev(d)) for d in range(1, N_TP)
        ]

    def send_section(slot, value):
        sx[slot] = value.astype(BF16)
        return [
            sender.start(sx.at[slot], rx.at[slot * 3, mine, :], sec_dev(N_SEC - 1, d))
            for d in range(N_TP)
        ]

    def mlp_forward(t, x):
        gain = gains[1:2, :]

        def norm(r):
            unit, _ = unit_of(x[0, pl.ds(r, 32), :])
            fl[NU, pl.ds(t * rows + r, 32), :] = (unit * gain).astype(BF16)

        loop(rows // 32, 32, norm)

    def mlp_hidden(t):
        def up(c):
            out = dot(fl[NU, pl.ds(t * rows, rows), :], wup[:, pl.ds(c, 256)], NN)
            pre[:, pl.ds(c, 256)] = out
            hidden[pl.ds(t * rows, rows), pl.ds(c, 256)] = gelu(out).astype(BF16)

        loop(hid // 256, 256, up)

    def mlp_down(t):
        def down(c):
            snd[t, 0, :, pl.ds(c, 256)] = dot(
                hidden[pl.ds(t * rows, rows), :], wdn[pl.ds(c, 256), :], NT
            ).astype(BF16)

        loop(width // 256, 256, down)

    def mlp_back(t, x):
        def low(r):
            fl[GL, pl.ds(t * rows + r, 32), :] = x[3, pl.ds(r, 32), :].astype(BF16)

        loop(rows // 32, 32, low)

        def back(c):
            grad = dot(fl[GL, pl.ds(t * rows, rows), :], wdn[:, pl.ds(c, 256)], NN)
            gp[pl.ds(t * rows, rows), pl.ds(c, 256)] = (
                grad * gelu_slope(pre[:, pl.ds(c, 256)])
            ).astype(BF16)

        loop(hid // 256, 256, back)

        def out(c):
            snd[t, 1, :, pl.ds(c, 256)] = dot(
                gp[pl.ds(t * rows, rows), :], wup[pl.ds(c, 256), :], NT
            ).astype(BF16)

        loop(width // 256, 256, out)

    def attention_in(t, x, slot):
        gain = gains[0:1, :]

        def low(r):
            value = x[1, pl.ds(r, 32), :] - ag[slot, pl.ds(r, 32), :].astype(F32)
            x[1, pl.ds(r, 32), :] = value
            if t == 0:
                rx_low[pl.ds(r, 32), :] = value.astype(BF16)
            unit, _ = unit_of(value)
            fl[AL, pl.ds(t * rows + r, 32), :] = (unit * gain).astype(BF16)

        rx_low = snd.at[0, 0]
        loop(rows // 32, 32, low)
        packed = dot(fl[AL, pl.ds(t * rows, rows), :], wkv[...].reshape(att, width), NT).astype(BF16)
        across, along = [], []
        for h in range(heads):
            kvb[t, h, 0, 0] = packed[:, h * PAIR : (h + 1) * PAIR]
            across.append(sender.start(kvb.at[t, h, 0, 0], kvb.at[t, h, 1, 0], seq_dev(N_Z)))
            along.append(
                [sender.start(kvb.at[t, h, 0, 0], kvb.at[t, h, 0, d], seq_dev(d)) for d in range(1, N_Z)]
            )
        query = dot(fl[AL, pl.ds(t * rows, rows), :], wqo[...].reshape(att, width), NT)
        query = query.astype(BF16).astype(F32) * 0.125
        qd[pl.ds(0, rows), :] = jnp.where(lane_all < HEAD_DIM, query, 0.0).astype(BF16)
        return across, along

    def pass_along(t, copies):
        across, along = copies
        late = []
        for h in range(KV_X_FIRST):
            received([across[h]])
            late.append(
                [sender.start(kvb.at[t, h, 1, 0], kvb.at[t, h, 1, d], seq_dev(d)) for d in range(1, N_Z)]
            )
        return late

    def pass_across(t, copies, late):
        across, along = copies
        for h in range(KV_X_FIRST, heads):
            received(along[h])
            late.append(
                [sender.start(kvb.at[t, h, 0, d], kvb.at[t, h, 1, d], seq_dev(N_Z)) for d in range(1, N_Z)]
            )
        return late

    def grads_in(t, x, slot):
        gain = gains[1:2, :]

        def total(r):
            grad = ag[slot, pl.ds(r, 32), :].astype(F32)
            value = x[2, pl.ds(r, 32), :] + norm_back(grad, gain, x[0, pl.ds(r, 32), :])
            x[2, pl.ds(r, 32), :] = value
            fl[TL, pl.ds(t * rows + r, 32), :] = value.astype(BF16)

        loop(rows // 32, 32, total)
        grad = dot(fl[TL, pl.ds(t * rows, rows), :], wqo[...].reshape(att, width), NT)
        qd[pl.ds(rows, rows), :] = jnp.where(lane_all >= HEAD_DIM, grad, 0.0).astype(BF16)

    def attend(t, copies, late):
        across, along = copies
        tokens = N_SEQ * rows
        first = []
        for h in range(heads):
            lanes = pl.ds(h * PAIR, PAIR)
            if h < KV_X_FIRST:
                received(along[h])
            else:
                received([across[h]])
            received(late[h])
            kv = kvb[t, h].reshape(tokens, PAIR)
            both = qd[:, lanes]
            scores[...] = dot(kv, both, NT)
            logits = scores[:, :rows]
            weight = jnp.exp(logits - jnp.max(logits, 0, keepdims=True))
            probs = weight * (1.0 / jnp.sum(weight, 0, keepdims=True))
            grad_probs = scores[:, rows:]
            delta = jnp.sum(probs * grad_probs, 0, keepdims=True)
            pd[:, rows:] = probs.astype(BF16)
            pd[:, :rows] = (probs * (grad_probs - delta)).astype(BF16)
            dks[t, h] = dot(pd[...], both, NN).astype(BF16).reshape(2, N_Z, rows, PAIR)
            if h < DKV_X_FIRST:
                first.append([sender.start(dks.at[t, h, 1], dax.at[t, h], seq_dev(N_Z))])
            else:
                first.append(
                    [
                        sender.start(dks.at[t, h, :, d], dbz.at[t, h - DKV_X_FIRST, d - 1], seq_back(d))
                        for d in range(1, N_Z)
                    ]
                )
            mixed = dot(pd[...], kv, TN)
            dqf[pl.ds(t * rows, rows), lanes] = jnp.where(lane < HEAD_DIM, mixed[:rows] * 0.125, 0.0).astype(BF16)
            mxf[pl.ds(t * rows, rows), lanes] = jnp.where(lane >= HEAD_DIM, mixed[rows:], 0.0).astype(BF16)
        return first

    def attention_out(t):
        def out(c):
            snd[t, 2, :, pl.ds(c, 256)] = dot(
                mxf[pl.ds(t * rows, rows), :], wqo[:, :, :, pl.ds(c, 256)].reshape(att, 256), NN
            ).astype(BF16)

        loop(width // 256, 256, out)
        return scatter(t, 2)

    def attention_relay(t, first):
        last = []
        for h in range(heads):
            received(first[h])
            if h < DKV_X_FIRST:
                for d in (1, 2, 3, 0):
                    dks[t, h, 0, d] = (
                        dks[t, h, 0, d].astype(F32) + dax[t, h, d].astype(F32)
                    ).astype(BF16)
                    if d > 0:
                        last.append(sender.start(dks.at[t, h, 0, d], daz.at[t, h, d - 1], seq_back(d)))
            else:
                k = h - DKV_X_FIRST
                for side in (1, 0):
                    total = dks[t, h, side, 0].astype(F32)
                    for d in range(N_Z - 1):
                        total = total + dbz[t, k, d, side].astype(F32)
                    dks[t, h, side, 0] = total.astype(BF16)
                last.append(sender.start(dks.at[t, h, 1, 0], dbx.at[t, k], seq_dev(N_Z)))
        return last

    def attention_back(t, last):
        received(last)
        for h in range(heads):
            total = dks[t, h, 0, 0].astype(F32)
            if h < DKV_X_FIRST:
                for d in range(N_Z - 1):
                    total = total + daz[t, h, d].astype(F32)
            else:
                total = total + dbx[t, h - DKV_X_FIRST].astype(F32)
            dkvf[pl.ds(t * rows, rows), pl.ds(h * PAIR, PAIR)] = total.astype(BF16)

        def out(c):
            cols = pl.ds(c, 256)
            snd[t, 3, :, cols] = (
                dot(dkvf[pl.ds(t * rows, rows), :], wkv[:, :, :, cols].reshape(att, 256), NN)
                + dot(dqf[pl.ds(t * rows, rows), :], wqo[:, :, :, cols].reshape(att, 256), NN)
            ).astype(BF16)

        loop(width // 256, 256, out)
        return scatter(t, 3)

    def grad_rows(by_x, by_z):
        index = lax.rem(x_hi + by_x, 2) * N_Z + lax.rem(z + by_z, N_Z)
        return pl.ds(pl.multiple_of(index * chunk, 32), chunk)

    def reduce_first(g, cut, ra, rb):
        other = pl.ds(pl.multiple_of((1 - x_hi) * half, 32), half)
        cols_a, cols_b = pl.ds(0, cut), pl.ds(cut, g.shape[1] - cut)
        first = [sender.start(g.at[other, cols_a], ra, seq_dev(N_Z))]
        second = []
        for d in range(1, N_Z):
            for k in range(2):
                second.append(sender.start(g.at[grad_rows(k, d), cols_b], rb.at[d - 1, k], seq_dev(d)))
        return first, second

    def reduce_second(g, cut, ra, rb, rz, rw, copies):
        first, second = copies
        cols_a, cols_b = pl.ds(0, cut), pl.ds(cut, g.shape[1] - cut)
        base = x_hi * half
        received(first)

        def add_a(r):
            here = pl.ds(pl.multiple_of(base + r, 32), 32)
            g[here, cols_a] = (g[here, cols_a].astype(F32) + ra[pl.ds(r, 32), :].astype(F32)).astype(BF16)

        loop(half // 32, 32, add_a)
        out = [
            sender.start(g.at[grad_rows(0, d), cols_a], rz.at[d - 1], seq_dev(d)) for d in range(1, N_Z)
        ]
        received(second)
        for k in (1, 0):
            start = (lax.rem(x_hi + k, 2) * N_Z + z) * chunk

            def add_b(r):
                here = pl.ds(pl.multiple_of(start + r, 32), 32)
                total = g[here, cols_b].astype(F32)
                for d in range(N_Z - 1):
                    total = total + rb[d, k, pl.ds(r, 32), :].astype(F32)
                g[here, cols_b] = total.astype(BF16)

            loop(chunk // 32, 32, add_b)
            if k == 1:
                out.append(sender.start(g.at[grad_rows(1, 0), cols_b], rw, seq_dev(N_Z)))
        return out

    def reduce_last(g, cut, rz, rw, store, copies):
        cols_a, cols_b = pl.ds(0, cut), pl.ds(cut, g.shape[1] - cut)
        received(copies)
        start = seq * chunk

        def add(r):
            here = pl.ds(pl.multiple_of(start + r, 32), 32)
            total = g[here, cols_a].astype(F32)
            for d in range(N_Z - 1):
                total = total + rz[d, pl.ds(r, 32), :].astype(F32)
            rest = g[here, cols_b].astype(F32) + rw[pl.ds(r, 32), :].astype(F32)
            store(pl.ds(r, 32), total.astype(BF16), rest.astype(BF16))

        loop(chunk // 32, 32, add)

    def store_mlp(here, left, right):
        om[0, here, :] = left[:, :hid]
        om[1, here, pl.ds(0, cut_mlp - hid)] = left[:, hid:]
        om[1, here, pl.ds(cut_mlp - hid, 2 * hid - cut_mlp)] = right

    def store_att(here, left, right):
        def piece(p, h, k):
            start = p * att + h * PAIR + k * HEAD_DIM
            if start < cut_att:
                return left[:, start : start + HEAD_DIM]
            return right[:, start - cut_att : start - cut_att + HEAD_DIM]

        def joined(p, k):
            return jnp.concatenate([piece(p, h, k) for h in range(heads)], 1)

        oqkv[0, here, :] = joined(1, 0)
        oqkv[1, here, :] = joined(0, 0)
        oqkv[2, here, :] = joined(0, 1)
        oout[here, :] = joined(1, 1)

    def grads_mlp():
        def tile(c):
            gmlp[pl.ds(c, 256), pl.ds(0, hid)] = dot(fl[NU, :, pl.ds(c, 256)], gp[...], TN).astype(BF16)
            gmlp[pl.ds(c, 256), pl.ds(hid, hid)] = dot(fl[GL, :, pl.ds(c, 256)], hidden[...], TN).astype(BF16)

        loop(width // 256, 256, tile)
        return reduce_first(gmlp, cut_mlp, ra_m, rb_m)

    def grads_att():
        def tile(c):
            left = fl[AL, :, pl.ds(c, 256)]
            gatt[pl.ds(c, 256), pl.ds(0, att)] = dot(left, dkvf[...], TN).astype(BF16)
            gatt[pl.ds(c, 256), pl.ds(att, att)] = (
                dot(left, dqf[...], TN) + dot(fl[TL, :, pl.ds(c, 256)], mxf[...], TN)
            ).astype(BF16)

        loop(width // 256, 256, tile)
        return reduce_first(gatt, cut_att, ra_a, rb_a)

    loads[0].wait()
    loads[1].wait()
    mlp_forward(0, xs)
    loads[2].wait()
    mlp_hidden(0)
    loads[3].wait()
    mlp_down(0)
    pl.semaphore_wait(barrier, N_TP - 1 + N_SEQ - 1 + N_TP)
    c_mlp = scatter(0, 0)
    mlp_back(0, xs)
    c_mlp = spread(0, summed(0, 0, c_mlp))
    received(c_mlp)
    c_grad = scatter(0, 1)
    for k in range(4, 8):
        loads[k].wait()
    for copy in sender.all[:3]:
        copy.wait_send()
    c_kv = attention_in(0, xs, 0)
    late = pass_along(0, c_kv)
    c_grad = spread(1, summed(0, 1, c_grad))
    late = pass_across(0, c_kv, late)
    received(c_grad)
    grads_in(0, xs, 1)
    c_dkv = attend(0, c_kv, late)
    c_att = attention_out(0)
    c_dkv = attention_relay(0, c_dkv)
    c_up = send_section(0, xs[0, mine, :] - summed(0, 2, c_att))
    c_low = sender.start(snd.at[0, 0], rx.at[1], sec_dev(N_SEC - 1, 0))
    c_total = sender.start(fl.at[TL, pl.ds(0, rows), :], rx.at[2], sec_dev(N_SEC - 1, 0))

    is_last = sec == N_SEC - 1
    loads[8].wait()

    def choose(k):
        def one(r):
            hd[k, pl.ds(r, 32), :] = jnp.where(
                is_last, hd[k, pl.ds(r, 32), :], rx[k, pl.ds(r, 32), :].astype(F32)
            )

        loop(rows // 32, 32, one)

    outs = []

    def emit(k):
        copy = pltpu.make_async_copy(hd.at[k], recon_h.at[k], out_sem.at[k])
        copy.start()
        outs.append(copy)

    def finish(src, dst, k):
        copy = pltpu.make_async_copy(src, dst, out_sem.at[k])
        copy.start()
        outs.append(copy)

    slope = gains[0:1, :]
    c_att = attention_back(0, c_dkv)
    received(c_up)
    choose(0)
    mlp_forward(1, hd)
    mlp_hidden(1)
    mlp_down(1)
    c_mlp = scatter(1, 0)
    grad = summed(0, 3, c_att)
    c_gl = send_section(1, xs[3, mine, :] + norm_back(grad, slope, xs[1, mine, :]))
    c_mlp = spread(2, summed(1, 0, c_mlp))
    received([c_low])
    choose(1)
    received(c_mlp)
    c_kv = attention_in(1, hd, 2)
    emit(1)
    received(c_gl)
    choose(3)
    late = pass_across(1, c_kv, pass_along(1, c_kv))
    mlp_back(1, hd)
    c_grad = scatter(1, 1)
    c_gm = grads_mlp()
    c_grad = spread(3, summed(1, 1, c_grad))
    received([c_total])
    choose(2)
    received(c_grad)
    grads_in(1, hd, 3)
    emit(2)
    c_dkv = attend(1, c_kv, late)
    c_att = attention_out(1)
    c_dkv = attention_relay(1, c_dkv)
    c_up = spread(4, summed(1, 2, c_att))
    c_att = attention_back(1, c_dkv)
    c_ga = grads_att()
    c_gl = spread(5, summed(1, 3, c_att))
    c_gm = reduce_second(gmlp, cut_mlp, ra_m, rb_m, rz_m, rw_m, c_gm)
    received(c_up)

    def upper(r):
        here = pl.ds(r, 32)
        value = hd[0, here, :]
        pre[here, :] = value - ag[4, here, :].astype(F32)

    loop(rows // 32, 32, upper)
    copy = pltpu.make_async_copy(pre, recon_h.at[0], out_sem.at[0])
    copy.start()
    outs.append(copy)
    received(c_gl)

    def lower(r):
        here = pl.ds(r, 32)
        hd[3, here, :] = hd[3, here, :] + norm_back(
            ag[5, here, :].astype(F32), slope, xs_low(here)
        )

    def xs_low(here):
        return hd[1, here, :]

    loop(rows // 32, 32, lower)
    emit(3)
    c_ga = reduce_second(gatt, cut_att, ra_a, rb_a, rz_a, rw_a, c_ga)
    reduce_last(gmlp, cut_mlp, rz_m, rw_m, store_mlp, c_gm)
    finish(om.at[0], gup_h, 4)
    finish(om.at[1], gdn_h, 5)
    reduce_last(gatt, cut_att, rz_a, rw_a, store_att, c_ga)
    finish(oqkv, gqkv_h, 6)
    finish(oout, gout_h, 7)
    for copy in sender.all[3:]:
        copy.wait_send()
    for copy in outs:
        copy.wait()


N_COPIES = 240


def per_device(streams, head_streams, gains, w_qkv, w_out, w_up, w_down):
    rows, width = streams.shape[2], streams.shape[3]
    hid = w_up.shape[2]
    local = w_out.shape[2]
    att = 2 * local
    heads = local // HEAD_DIM
    chunk = width // N_SEQ
    half = width // 2
    cut_mlp = 1536
    cut_att = 768
    wqkv = jnp.transpose(w_qkv[0], (1, 2, 0)).reshape(3, heads, HEAD_DIM, width)
    wout = jnp.transpose(w_out[0], (1, 0)).reshape(heads, HEAD_DIM, width)
    sizes = (rows, width, hid, att, cut_mlp, cut_att)
    quarter = rows // N_TP
    rest_m, rest_a = 2 * hid - cut_mlp, 2 * att - cut_att
    n_dx, n_dz = DKV_X_FIRST, heads - DKV_X_FIRST
    vm = pltpu.VMEM
    scratch = [
        vm((4, rows, width), F32), vm((4, rows, width), F32), vm((2, width), F32),
        vm((heads, 2, HEAD_DIM, width), BF16), vm((heads, 2, HEAD_DIM, width), BF16),
        vm((width, hid), BF16), vm((width, hid), BF16),
        vm((4, rows, width), BF16), vm((2, quarter, width), BF16),
        vm((4, 2 * rows, width), BF16), vm((2 * rows, hid), BF16), vm((2 * rows, hid), BF16),
        vm((2 * rows, att), BF16), vm((2 * rows, att), BF16), vm((2 * rows, att), BF16),
        vm((2, 4, rows, width), BF16), vm((2, 4, N_TP - 1, quarter, width), BF16), vm((6, rows, width), BF16),
        vm((2, heads, 2, N_Z, rows, PAIR), BF16), vm((2, heads, 2, N_Z, rows, PAIR), BF16),
        vm((2, n_dx, N_Z, rows, PAIR), BF16), vm((2, n_dx, N_Z - 1, rows, PAIR), BF16),
        vm((2, n_dz, N_Z - 1, 2, rows, PAIR), BF16), vm((2, n_dz, rows, PAIR), BF16),
        vm((rows, hid), F32), vm((2 * rows, att), BF16),
        vm((N_SEQ * rows, 2 * rows), F32), vm((N_SEQ * rows, 2 * rows), BF16),
        vm((width, 2 * hid), BF16), vm((width, 2 * att), BF16),
        vm((half, cut_mlp), BF16), vm((N_Z - 1, chunk, cut_mlp), BF16),
        vm((N_Z - 1, 2, chunk, rest_m), BF16), vm((chunk, rest_m), BF16),
        vm((half, cut_att), BF16), vm((N_Z - 1, chunk, cut_att), BF16),
        vm((N_Z - 1, 2, chunk, rest_a), BF16), vm((chunk, rest_a), BF16),
        vm((2, chunk, hid), BF16), vm((3, chunk, local), BF16), vm((chunk, local), BF16),
        pltpu.SemaphoreType.DMA((9,)), pltpu.SemaphoreType.DMA((8,)),
        pltpu.SemaphoreType.DMA((N_COPIES,)), pltpu.SemaphoreType.DMA((N_COPIES,)),
    ]
    any_spec = pl.BlockSpec(memory_space=pl.ANY)
    recon, grad_qkv, grad_out, grad_up, grad_down = pl.pallas_call(
        lambda *refs: kernel(sizes, *refs),
        out_shape=(
            jax.ShapeDtypeStruct((4, rows, width), F32),
            jax.ShapeDtypeStruct((3, chunk, local), BF16),
            jax.ShapeDtypeStruct((chunk, local), BF16),
            jax.ShapeDtypeStruct((chunk, hid), BF16),
            jax.ShapeDtypeStruct((chunk, hid), BF16),
        ),
        in_specs=[any_spec] * 7,
        out_specs=(any_spec,) * 5,
        scratch_shapes=scratch,
        compiler_params=pltpu.CompilerParams(
            collective_id=0, has_side_effects=True, vmem_limit_bytes=67043328
        ),
        name="window",
    )(streams[0], head_streams, gains[0], wqkv, wout, w_up[0], w_down[0])
    grad_qkv = jnp.transpose(grad_qkv, (1, 0, 2))
    return (recon[None], grad_qkv[None], grad_out[None], grad_up[None], grad_down[None])


def solution(mesh):
    return jax.shard_map(
        per_device,
        mesh=mesh,
        in_specs=(
            P("section", None, "seq", None),
            P(None, "seq", None),
            P("section", None, None),
            P("section", None, None, "tp"),
            P("section", None, "tp"),
            P("section", None, "tp"),
            P("section", None, "tp"),
        ),
        out_specs=(
            P("section", None, "seq", None),
            P("section", "seq", None, "tp"),
            P("section", "seq", "tp"),
            P("section", "seq", "tp"),
            P("section", "seq", "tp"),
        ),
        check_vma=False,
    )
```

```python
import math

import jax
import jax.numpy as jnp
from jax import lax
from jax.experimental import pallas as pl
from jax.experimental.pallas import tpu as pltpu
from jax.sharding import PartitionSpec as P

MESH = pl.DeviceIdType.MESH
BF16 = jnp.bfloat16
F32 = jnp.float32
HEAD_DIM = 64
PAIR = 2 * HEAD_DIM
N_TP = 4
N_Z = 4
N_SEQ = 8
N_SEC = 4
KV_X_FIRST = 2
DKV_X_FIRST = 3
HIDDEN_X_FIRST = 768
NU, GL, AL, TL = 0, 1, 2, 3
NN = (((1,), (0,)), ((), ()))
NT = (((1,), (1,)), ((), ()))
TN = (((0,), (0,)), ((), ()))


def dot(a, b, dims):
    return lax.dot_general(a, b, dims, preferred_element_type=F32)


def loop(count, size, body):
    def step(i, carry):
        body(pl.multiple_of(i * size, size))
        return carry

    lax.fori_loop(0, count, step, 0)


def unit_of(values):
    centre = values - jnp.mean(values, -1, keepdims=True)
    inv_std = lax.rsqrt(jnp.mean(centre * centre, -1, keepdims=True) + 1e-06)
    return centre * inv_std, inv_std


def norm_back(grad, gain, values):
    unit, inv_std = unit_of(values)
    scaled = grad * gain
    return inv_std * (
        scaled
        - jnp.mean(scaled, -1, keepdims=True)
        - unit * jnp.mean(scaled * unit, -1, keepdims=True)
    )


GELU_C = math.sqrt(2.0 / math.pi)


def gelu(x):
    return 0.5 * x * (1.0 + jnp.tanh(GELU_C * (x + 0.044715 * (x * x * x))))


def gelu_slope(x):
    t = jnp.tanh(GELU_C * (x + 0.044715 * (x * x * x)))
    return 0.5 * (1.0 + t) + 0.5 * x * (1.0 - t * t) * (GELU_C * (1.0 + 0.134145 * (x * x)))


class Sender:
    def __init__(self, send_sem, recv_sem):
        self.send_sem, self.recv_sem = send_sem, recv_sem
        self.all = []

    def start(self, src, dst, device):
        k = len(self.all)
        copy = pltpu.make_async_remote_copy(
            src_ref=src,
            dst_ref=dst,
            send_sem=self.send_sem.at[k],
            recv_sem=self.recv_sem.at[k],
            device_id=device,
            device_id_type=MESH,
        )
        copy.start()
        self.all.append(copy)
        return copy


def received(copies):
    for copy in copies:
        copy.wait_recv()


def kernel(sizes, *refs):
    rows, width, hid, att, cut_mlp, cut_att = sizes
    (streams_h, head_h, gains_h, wqkv_h, wout_h, wup_h, wdn_h) = refs[:7]
    (recon_h, gqkv_h, gout_h, gup_h, gdn_h) = refs[7:12]
    (
        xs, hd, gains, wkv, wqo, wup, wdn,
        rx, sx, fl, gp, hall, glt, gsl, dkvf, dqf, mxf,
        snd, rr, ag, kvb, dks, dax, daz, dbz, dbx, pre, qd, scores, pd,
        gmlp, gatt, gkv, ra_m, rz_m, rb_m, rw_m, ra_a, rz_a, rb_a, rw_a,
        ra_k, rz_k, rb_k, rw_k, om, oqkv, oout,
        load_sem, out_sem, send_sem, recv_sem,
    ) = refs[12:]
    heads = att // PAIR
    sec = lax.axis_index("section")
    seq = lax.axis_index("seq")
    tp = lax.axis_index("tp")
    x_hi, z = seq // N_Z, lax.rem(seq, N_Z)
    quarter = rows // N_TP
    chunk = width // N_SEQ
    half = width // 2
    mine = pl.ds(pl.multiple_of(tp * quarter, quarter), quarter)

    def tp_dev(d):
        return {"tp": lax.rem(tp + d, N_TP)}

    def seq_dev(d):
        return {"seq": lax.rem(x_hi + d // N_Z, 2) * N_Z + lax.rem(z + d % N_Z, N_Z)}

    def seq_back(d):
        return {"seq": lax.rem(x_hi + d // N_Z, 2) * N_Z + lax.rem(z + N_Z - d % N_Z, N_Z)}

    def sec_dev(by, d):
        return {"section": lax.rem(sec + by, N_SEC), "tp": lax.rem(tp + d, N_TP)}

    barrier = pltpu.get_barrier_semaphore()
    for d in range(1, N_TP):
        pl.semaphore_signal(barrier, inc=1, device_id=tp_dev(d), device_id_type=MESH)
    for d in range(1, N_SEQ):
        pl.semaphore_signal(barrier, inc=1, device_id=seq_dev(d), device_id_type=MESH)
    for d in range(N_TP):
        pl.semaphore_signal(barrier, inc=1, device_id=sec_dev(1, d), device_id_type=MESH)

    moves = (
        (gains_h, gains), (streams_h.at[0], xs.at[0]), (wup_h, wup), (wdn_h, wdn),
        (streams_h.at[3], xs.at[3]), (streams_h.at[1], xs.at[1]), (streams_h.at[2], xs.at[2]),
        (wqkv_h.at[1], wkv.at[:, 0]), (wqkv_h.at[2], wkv.at[:, 1]),
        (wqkv_h.at[0], wqo.at[:, 0]), (wout_h, wqo.at[:, 1]), (head_h, hd),
    )
    loads = []

    def load(count):
        for src, dst in moves[len(loads) : len(loads) + count]:
            copy = pltpu.make_async_copy(src, dst, load_sem.at[len(loads)])
            copy.start()
            loads.append(copy)

    load(5)
    sender = Sender(send_sem, recv_sem)

    lane = lax.broadcasted_iota(jnp.int32, (rows, PAIR), 1)
    lane_all = lax.rem(lax.broadcasted_iota(jnp.int32, (rows, att), 1), PAIR)

    def peer_rows(d):
        return pl.ds(pl.multiple_of(lax.rem(tp + d, N_TP) * quarter, quarter), quarter)

    def scatter(t, k):
        return [
            sender.start(snd.at[t, k, peer_rows(d), :], rr.at[t, k, d - 1], tp_dev(d))
            for d in range(1, N_TP)
        ]

    def summed(t, k, copies):
        received(copies)
        total = snd[t, k, mine, :].astype(F32)
        for d in range(N_TP - 1):
            total = total + rr[t, k, d].astype(F32)
        return total

    def spread(slot, value):
        ag[slot, mine, :] = value.astype(BF16)
        return [
            sender.start(ag.at[slot, mine, :], ag.at[slot, mine, :], tp_dev(d)) for d in range(1, N_TP)
        ]

    def send_section(slot, value):
        sx[slot] = value.astype(BF16)
        return [
            sender.start(sx.at[slot], rx.at[slot * 3, mine, :], sec_dev(N_SEC - 1, d))
            for d in range(N_TP)
        ]

    def mlp_forward(t, x):
        gain = gains[1:2, :]

        def norm(r):
            unit, _ = unit_of(x[0, pl.ds(r, 32), :])
            fl[NU, pl.ds(t * rows + r, 32), :] = (unit * gain).astype(BF16)

        loop(rows // 32, 32, norm)

    def mlp_hidden(t):
        def up(c):
            out = dot(fl[NU, pl.ds(t * rows, rows), :], wup[:, pl.ds(c, 256)], NN)
            pre[:, pl.ds(c, 256)] = out
            hall[t, 0, 0, :, pl.ds(c, 256)] = gelu(out).astype(BF16)

        loop(hid // 256, 256, up)

    def mlp_down(t):
        def down(c):
            snd[t, 0, :, pl.ds(c, 256)] = dot(
                hall[t, 0, 0], wdn[pl.ds(c, 256), :], NT
            ).astype(BF16)

        loop(width // 256, 256, down)

    def mlp_back(t, x):
        def low(r):
            fl[GL, pl.ds(t * rows + r, 32), :] = x[3, pl.ds(r, 32), :].astype(BF16)

        loop(rows // 32, 32, low)

        def back(c):
            grad = dot(fl[GL, pl.ds(t * rows, rows), :], wdn[:, pl.ds(c, 256)], NN)
            gp[pl.ds(t * rows, rows), pl.ds(c, 256)] = (
                grad * gelu_slope(pre[:, pl.ds(c, 256)])
            ).astype(BF16)

        loop(hid // 256, 256, back)

        def out(c):
            snd[t, 1, :, pl.ds(c, 256)] = dot(
                gp[pl.ds(t * rows, rows), :], wup[pl.ds(c, 256), :], NT
            ).astype(BF16)

        loop(width // 256, 256, out)

    def share(ref, t, cut):
        own, size = ref.at[t, 0, 0], ref.shape[4]
        left, right = pl.ds(0, cut), pl.ds(cut, size - cut)
        across = sender.start(own.at[:, left], ref.at[t, 1, 0, :, left], seq_dev(N_Z))
        along = [sender.start(own, ref.at[t, 0, d], seq_dev(d)) for d in range(1, N_Z)]
        rest = sender.start(own.at[:, right], ref.at[t, 1, 0, :, right], seq_dev(N_Z))
        return across, along, rest

    def share_pass(ref, t, cut, copies):
        across, along, rest = copies
        left, right = pl.ds(0, cut), pl.ds(cut, ref.shape[4] - cut)
        received([across])
        late = [
            sender.start(ref.at[t, 1, 0, :, left], ref.at[t, 1, d, :, left], seq_dev(d))
            for d in range(1, N_Z)
        ]
        received(along)
        late += [
            sender.start(ref.at[t, 0, d, :, right], ref.at[t, 1, d, :, right], seq_dev(N_Z))
            for d in range(1, N_Z)
        ]
        return late + [rest]

    def slices_out(t, factor, turned, gathered):
        def turn(c):
            tile = fl[factor, pl.ds(t * rows, rows), pl.ds(c, 128)]
            turned[t, pl.ds(c, 128), :] = tile.astype(F32).T.astype(BF16)

        loop(width // 128, 128, turn)
        gathered[:, pl.ds(t * N_SEQ * rows, rows)] = turned[t, grad_rows(0, 0), :]
        return [
            sender.start(
                turned.at[t, grad_rows(d // N_Z, d % N_Z), :],
                gathered.at[:, pl.ds((t * N_SEQ + d) * rows, rows)],
                seq_dev(d),
            )
            for d in range(1, N_SEQ)
        ]

    def grads_down(copies):
        received(copies)

        def tile(c):
            cols = pl.ds(c, 256)
            om[1, :, cols] = dot(
                gsl[...], hall[:, :, :, :, cols].reshape(2 * N_SEQ * rows, 256), NN
            ).astype(BF16)

        loop(hid // 256, 256, tile)

    def attention_in(t, x, slot):
        gain = gains[0:1, :]

        def low(r):
            value = x[1, pl.ds(r, 32), :] - ag[slot, pl.ds(r, 32), :].astype(F32)
            x[1, pl.ds(r, 32), :] = value
            if t == 0:
                rx_low[pl.ds(r, 32), :] = value.astype(BF16)
            unit, _ = unit_of(value)
            fl[AL, pl.ds(t * rows + r, 32), :] = (unit * gain).astype(BF16)

        rx_low = snd.at[0, 0]
        loop(rows // 32, 32, low)
        packed = dot(fl[AL, pl.ds(t * rows, rows), :], wkv[...].reshape(att, width), NT).astype(BF16)
        across, along = [], []
        for h in range(heads):
            kvb[t, h, 0, 0] = packed[:, h * PAIR : (h + 1) * PAIR]
            across.append(sender.start(kvb.at[t, h, 0, 0], kvb.at[t, h, 1, 0], seq_dev(N_Z)))
            along.append(
                [sender.start(kvb.at[t, h, 0, 0], kvb.at[t, h, 0, d], seq_dev(d)) for d in range(1, N_Z)]
            )
        query = dot(fl[AL, pl.ds(t * rows, rows), :], wqo[...].reshape(att, width), NT)
        query = query.astype(BF16).astype(F32) * 0.125
        qd[pl.ds(0, rows), :] = jnp.where(lane_all < HEAD_DIM, query, 0.0).astype(BF16)
        return across, along

    def pass_along(t, copies):
        across, along = copies
        late = []
        for h in range(KV_X_FIRST):
            received([across[h]])
            late.append(
                [sender.start(kvb.at[t, h, 1, 0], kvb.at[t, h, 1, d], seq_dev(d)) for d in range(1, N_Z)]
            )
        return late

    def pass_across(t, copies, late):
        across, along = copies
        for h in range(KV_X_FIRST, heads):
            received(along[h])
            late.append(
                [sender.start(kvb.at[t, h, 0, d], kvb.at[t, h, 1, d], seq_dev(N_Z)) for d in range(1, N_Z)]
            )
        return late

    def grads_in(t, x, slot):
        gain = gains[1:2, :]

        def total(r):
            grad = ag[slot, pl.ds(r, 32), :].astype(F32)
            value = x[2, pl.ds(r, 32), :] + norm_back(grad, gain, x[0, pl.ds(r, 32), :])
            x[2, pl.ds(r, 32), :] = value
            fl[TL, pl.ds(t * rows + r, 32), :] = value.astype(BF16)

        loop(rows // 32, 32, total)
        grad = dot(fl[TL, pl.ds(t * rows, rows), :], wqo[...].reshape(att, width), NT)
        qd[pl.ds(rows, rows), :] = jnp.where(lane_all >= HEAD_DIM, grad, 0.0).astype(BF16)

    def attend(t, copies, late):
        across, along = copies
        tokens = N_SEQ * rows
        first = []
        for h in range(heads):
            lanes = pl.ds(h * PAIR, PAIR)
            if h < KV_X_FIRST:
                received(along[h])
            else:
                received([across[h]])
            received(late[h])
            kv = kvb[t, h].reshape(tokens, PAIR)
            both = qd[:, lanes]
            scores[...] = dot(kv, both, NT)
            logits = scores[:, :rows]
            weight = jnp.exp(logits - jnp.max(logits, 0, keepdims=True))
            probs = weight * (1.0 / jnp.sum(weight, 0, keepdims=True))
            grad_probs = scores[:, rows:]
            delta = jnp.sum(probs * grad_probs, 0, keepdims=True)
            pd[:, rows:] = probs.astype(BF16)
            pd[:, :rows] = (probs * (grad_probs - delta)).astype(BF16)
            dks[t, h] = dot(pd[...], both, NN).astype(BF16).reshape(2, N_Z, rows, PAIR)
            if h < DKV_X_FIRST:
                first.append([sender.start(dks.at[t, h, 1], dax.at[t, h], seq_dev(N_Z))])
            else:
                first.append(
                    [
                        sender.start(dks.at[t, h, :, d], dbz.at[t, h - DKV_X_FIRST, d - 1], seq_back(d))
                        for d in range(1, N_Z)
                    ]
                )
            mixed = dot(pd[...], kv, TN)
            dqf[pl.ds(t * rows, rows), lanes] = jnp.where(lane < HEAD_DIM, mixed[:rows] * 0.125, 0.0).astype(BF16)
            mxf[pl.ds(t * rows, rows), lanes] = jnp.where(lane >= HEAD_DIM, mixed[rows:], 0.0).astype(BF16)
        return first

    def attention_out(t):
        def out(c):
            snd[t, 2, :, pl.ds(c, 256)] = dot(
                mxf[pl.ds(t * rows, rows), :], wqo[:, :, :, pl.ds(c, 256)].reshape(att, 256), NN
            ).astype(BF16)

        loop(width // 256, 256, out)
        return scatter(t, 2)

    def attention_relay(t, first):
        last = []
        for h in range(heads):
            received(first[h])
            if h < DKV_X_FIRST:
                for d in (1, 2, 3, 0):
                    dks[t, h, 0, d] = (
                        dks[t, h, 0, d].astype(F32) + dax[t, h, d].astype(F32)
                    ).astype(BF16)
                    if d > 0:
                        last.append(sender.start(dks.at[t, h, 0, d], daz.at[t, h, d - 1], seq_back(d)))
            else:
                k = h - DKV_X_FIRST
                for side in (1, 0):
                    total = dks[t, h, side, 0].astype(F32)
                    for d in range(N_Z - 1):
                        total = total + dbz[t, k, d, side].astype(F32)
                    dks[t, h, side, 0] = total.astype(BF16)
                last.append(sender.start(dks.at[t, h, 1, 0], dbx.at[t, k], seq_dev(N_Z)))
        return last

    def attention_back(t, last):
        received(last)
        for h in range(heads):
            total = dks[t, h, 0, 0].astype(F32)
            if h < DKV_X_FIRST:
                for d in range(N_Z - 1):
                    total = total + daz[t, h, d].astype(F32)
            else:
                total = total + dbx[t, h - DKV_X_FIRST].astype(F32)
            dkvf[pl.ds(t * rows, rows), pl.ds(h * PAIR, PAIR)] = total.astype(BF16)

        def out(c):
            cols = pl.ds(c, 256)
            snd[t, 3, :, cols] = (
                dot(dkvf[pl.ds(t * rows, rows), :], wkv[:, :, :, cols].reshape(att, 256), NN)
                + dot(dqf[pl.ds(t * rows, rows), :], wqo[:, :, :, cols].reshape(att, 256), NN)
            ).astype(BF16)

        loop(width // 256, 256, out)
        return scatter(t, 3)

    def grad_rows(by_x, by_z):
        index = lax.rem(x_hi + by_x, 2) * N_Z + lax.rem(z + by_z, N_Z)
        return pl.ds(pl.multiple_of(index * chunk, 32), chunk)

    def reduce_first(g, cut, ra, rb):
        other = pl.ds(pl.multiple_of((1 - x_hi) * half, 32), half)
        cols_a, cols_b = pl.ds(0, cut), pl.ds(cut, g.shape[1] - cut)
        first = [sender.start(g.at[other, cols_a], ra, seq_dev(N_Z))]
        second = []
        for d in range(1, N_Z):
            for k in range(2):
                second.append(sender.start(g.at[grad_rows(k, d), cols_b], rb.at[d - 1, k], seq_dev(d)))
        return first, second

    def reduce_second(g, cut, ra, rb, rz, rw, copies):
        first, second = copies
        cols_a, cols_b = pl.ds(0, cut), pl.ds(cut, g.shape[1] - cut)
        base = x_hi * half
        received(first)

        def add_a(r):
            here = pl.ds(pl.multiple_of(base + r, 32), 32)
            g[here, cols_a] = (g[here, cols_a].astype(F32) + ra[pl.ds(r, 32), :].astype(F32)).astype(BF16)

        loop(half // 32, 32, add_a)
        out = [
            sender.start(g.at[grad_rows(0, d), cols_a], rz.at[d - 1], seq_dev(d)) for d in range(1, N_Z)
        ]
        received(second)
        for k in (1, 0):
            start = (lax.rem(x_hi + k, 2) * N_Z + z) * chunk

            def add_b(r):
                here = pl.ds(pl.multiple_of(start + r, 32), 32)
                total = g[here, cols_b].astype(F32)
                for d in range(N_Z - 1):
                    total = total + rb[d, k, pl.ds(r, 32), :].astype(F32)
                g[here, cols_b] = total.astype(BF16)

            loop(chunk // 32, 32, add_b)
            if k == 1:
                out.append(sender.start(g.at[grad_rows(1, 0), cols_b], rw, seq_dev(N_Z)))
        return out

    def reduce_last(g, cut, rz, rw, store, copies):
        cols_a, cols_b = pl.ds(0, cut), pl.ds(cut, g.shape[1] - cut)
        received(copies)
        start = seq * chunk

        def add(r):
            here = pl.ds(pl.multiple_of(start + r, 32), 32)
            total = g[here, cols_a].astype(F32)
            for d in range(N_Z - 1):
                total = total + rz[d, pl.ds(r, 32), :].astype(F32)
            rest = g[here, cols_b].astype(F32) + rw[pl.ds(r, 32), :].astype(F32)
            store(pl.ds(r, 32), total.astype(BF16), rest.astype(BF16))

        loop(chunk // 32, 32, add)

    def store_mlp(here, left, right):
        om[0, here, pl.ds(0, cut_mlp)] = left
        om[0, here, pl.ds(cut_mlp, hid - cut_mlp)] = right

    def joined(left, right, k):
        pieces = []
        for h in range(heads):
            start = h * PAIR + k * HEAD_DIM
            if start < cut_att:
                pieces.append(left[:, start : start + HEAD_DIM])
            else:
                pieces.append(right[:, start - cut_att : start - cut_att + HEAD_DIM])
        return jnp.concatenate(pieces, 1)

    def store_qo(here, left, right):
        oqkv[0, here, :] = joined(left, right, 0)
        oout[here, :] = joined(left, right, 1)

    def store_kv(here, left, right):
        oqkv[1, here, :] = joined(left, right, 0)
        oqkv[2, here, :] = joined(left, right, 1)

    def grads_mlp():
        def tile(c):
            gmlp[pl.ds(c, 256), :] = dot(fl[NU, :, pl.ds(c, 256)], gp[...], TN).astype(BF16)

        loop(width // 256, 256, tile)
        return reduce_first(gmlp, cut_mlp, ra_m, rb_m)

    def grads_att():
        def tile(c):
            gatt[pl.ds(c, 256), :] = (
                dot(fl[AL, :, pl.ds(c, 256)], dqf[...], TN) + dot(fl[TL, :, pl.ds(c, 256)], mxf[...], TN)
            ).astype(BF16)

        loop(width // 256, 256, tile)
        return reduce_first(gatt, cut_att, ra_a, rb_a)

    def grads_kv():
        def tile(c):
            gkv[pl.ds(c, 256), :] = dot(fl[AL, :, pl.ds(c, 256)], dkvf[...], TN).astype(BF16)

        loop(width // 256, 256, tile)
        return reduce_first(gkv, cut_att, ra_k, rb_k)

    loads[0].wait()
    loads[1].wait()
    mlp_forward(0, xs)
    loads[2].wait()
    mlp_hidden(0)
    pl.semaphore_wait(barrier, N_TP - 1 + N_SEQ - 1 + N_TP)
    c_hid = share(hall, 0, HIDDEN_X_FIRST)
    loads[3].wait()
    load(7)
    mlp_down(0)
    c_mlp = c_first = scatter(0, 0)
    loads[4].wait()
    mlp_back(0, xs)
    c_mlp = spread(0, summed(0, 0, c_mlp))
    received(c_mlp)
    c_grad = scatter(0, 1)
    for k in range(5, 11):
        loads[k].wait()
    for copy in c_first:
        copy.wait_send()
    c_kv = attention_in(0, xs, 0)
    late = pass_along(0, c_kv)
    c_grad = spread(1, summed(0, 1, c_grad))
    late = pass_across(0, c_kv, late)
    received(c_grad)
    grads_in(0, xs, 1)
    c_dkv = attend(0, c_kv, late)
    c_att = attention_out(0)
    c_dkv = attention_relay(0, c_dkv)
    c_up = send_section(0, xs[0, mine, :] - summed(0, 2, c_att))
    c_low = sender.start(snd.at[0, 0], rx.at[1], sec_dev(N_SEC - 1, 0))
    c_total = sender.start(fl.at[TL, pl.ds(0, rows), :], rx.at[2], sec_dev(N_SEC - 1, 0))
    c_down = share_pass(hall, 0, HIDDEN_X_FIRST, c_hid) + slices_out(0, GL, glt, gsl)

    is_last = sec == N_SEC - 1
    loads[11].wait()

    def choose(k):
        def one(r):
            hd[k, pl.ds(r, 32), :] = jnp.where(
                is_last, hd[k, pl.ds(r, 32), :], rx[k, pl.ds(r, 32), :].astype(F32)
            )

        loop(rows // 32, 32, one)

    outs = []

    def emit(k):
        copy = pltpu.make_async_copy(hd.at[k], recon_h.at[k], out_sem.at[k])
        copy.start()
        outs.append(copy)

    def finish(src, dst, k):
        copy = pltpu.make_async_copy(src, dst, out_sem.at[k])
        copy.start()
        outs.append(copy)

    slope = gains[0:1, :]
    c_att = attention_back(0, c_dkv)
    received(c_up)
    choose(0)
    mlp_forward(1, hd)
    mlp_hidden(1)
    mlp_down(1)
    c_mlp = scatter(1, 0)
    c_hid = share(hall, 1, HIDDEN_X_FIRST)
    grad = summed(0, 3, c_att)
    c_gl = send_section(1, xs[3, mine, :] + norm_back(grad, slope, xs[1, mine, :]))
    c_mlp = spread(2, summed(1, 0, c_mlp))
    received([c_low])
    choose(1)
    received(c_mlp)
    c_kv = attention_in(1, hd, 2)
    emit(1)
    received(c_gl)
    choose(3)
    mlp_back(1, hd)
    c_grad = scatter(1, 1)
    late = pass_along(1, c_kv)
    c_gm = grads_mlp()
    late = pass_across(1, c_kv, late)
    c_grad = spread(3, summed(1, 1, c_grad))
    received([c_total])
    choose(2)
    c_down += slices_out(1, GL, glt, gsl)
    c_down += share_pass(hall, 1, HIDDEN_X_FIRST, c_hid)
    received(c_grad)
    grads_in(1, hd, 3)
    emit(2)
    c_dkv = attend(1, c_kv, late)
    c_att = attention_out(1)
    c_dkv = attention_relay(1, c_dkv)
    c_gm = reduce_second(gmlp, cut_mlp, ra_m, rb_m, rz_m, rw_m, c_gm)
    c_ga = grads_att()
    c_up = spread(4, summed(1, 2, c_att))
    c_att = attention_back(1, c_dkv)
    c_gk = grads_kv()
    c_gl = spread(5, summed(1, 3, c_att))
    received(c_up)

    def upper(r):
        here = pl.ds(r, 32)
        value = hd[0, here, :]
        pre[here, :] = value - ag[4, here, :].astype(F32)

    loop(rows // 32, 32, upper)
    copy = pltpu.make_async_copy(pre, recon_h.at[0], out_sem.at[0])
    copy.start()
    outs.append(copy)
    received(c_gl)

    def lower(r):
        here = pl.ds(r, 32)
        hd[3, here, :] = hd[3, here, :] + norm_back(
            ag[5, here, :].astype(F32), slope, xs_low(here)
        )

    def xs_low(here):
        return hd[1, here, :]

    loop(rows // 32, 32, lower)
    emit(3)
    c_ga = reduce_second(gatt, cut_att, ra_a, rb_a, rz_a, rw_a, c_ga)
    grads_down(c_down)
    finish(om.at[1], gdn_h, 5)
    reduce_last(gmlp, cut_mlp, rz_m, rw_m, store_mlp, c_gm)
    finish(om.at[0], gup_h, 4)
    c_gk = reduce_second(gkv, cut_att, ra_k, rb_k, rz_k, rw_k, c_gk)
    reduce_last(gatt, cut_att, rz_a, rw_a, store_qo, c_ga)
    finish(oout, gout_h, 7)
    reduce_last(gkv, cut_att, rz_k, rw_k, store_kv, c_gk)
    finish(oqkv, gqkv_h, 6)
    for copy in [c for c in sender.all if all(c is not f for f in c_first)]:
        copy.wait_send()
    for copy in outs:
        copy.wait()


N_COPIES = 312


def per_device(streams, head_streams, gains, w_qkv, w_out, w_up, w_down):
    rows, width = streams.shape[2], streams.shape[3]
    hid = w_up.shape[2]
    local = w_out.shape[2]
    att = 2 * local
    heads = local // HEAD_DIM
    chunk = width // N_SEQ
    half = width // 2
    cut_mlp = 768
    cut_att = 384
    wqkv = jnp.transpose(w_qkv[0], (1, 2, 0)).reshape(3, heads, HEAD_DIM, width)
    wout = jnp.transpose(w_out[0], (1, 0)).reshape(heads, HEAD_DIM, width)
    sizes = (rows, width, hid, att, cut_mlp, cut_att)
    quarter = rows // N_TP
    rest_m, rest_a = hid - cut_mlp, att - cut_att
    n_dx, n_dz = DKV_X_FIRST, heads - DKV_X_FIRST
    vm = pltpu.VMEM
    scratch = [
        vm((4, rows, width), F32), vm((4, rows, width), F32), vm((2, width), F32),
        vm((heads, 2, HEAD_DIM, width), BF16), vm((heads, 2, HEAD_DIM, width), BF16),
        vm((width, hid), BF16), vm((width, hid), BF16),
        vm((4, rows, width), BF16), vm((2, quarter, width), BF16),
        vm((4, 2 * rows, width), BF16), vm((2 * rows, hid), BF16),
        vm((2, 2, N_Z, rows, hid), BF16), vm((2, width, rows), BF16), vm((chunk, 2 * N_SEQ * rows), BF16),
        vm((2 * rows, att), BF16), vm((2 * rows, att), BF16), vm((2 * rows, att), BF16),
        vm((2, 4, rows, width), BF16), vm((2, 4, N_TP - 1, quarter, width), BF16), vm((6, rows, width), BF16),
        vm((2, heads, 2, N_Z, rows, PAIR), BF16), vm((2, heads, 2, N_Z, rows, PAIR), BF16),
        vm((2, n_dx, N_Z, rows, PAIR), BF16), vm((2, n_dx, N_Z - 1, rows, PAIR), BF16),
        vm((2, n_dz, N_Z - 1, 2, rows, PAIR), BF16), vm((2, n_dz, rows, PAIR), BF16),
        vm((rows, hid), F32), vm((2 * rows, att), BF16),
        vm((N_SEQ * rows, 2 * rows), F32), vm((N_SEQ * rows, 2 * rows), BF16),
        vm((width, hid), BF16), vm((width, att), BF16), vm((width, att), BF16),
        vm((half, cut_mlp), BF16), vm((N_Z - 1, chunk, cut_mlp), BF16),
        vm((N_Z - 1, 2, chunk, rest_m), BF16), vm((chunk, rest_m), BF16),
        vm((half, cut_att), BF16), vm((N_Z - 1, chunk, cut_att), BF16),
        vm((N_Z - 1, 2, chunk, rest_a), BF16), vm((chunk, rest_a), BF16),
        vm((half, cut_att), BF16), vm((N_Z - 1, chunk, cut_att), BF16),
        vm((N_Z - 1, 2, chunk, rest_a), BF16), vm((chunk, rest_a), BF16),
        vm((2, chunk, hid), BF16), vm((3, chunk, local), BF16), vm((chunk, local), BF16),
        pltpu.SemaphoreType.DMA((12,)), pltpu.SemaphoreType.DMA((8,)),
        pltpu.SemaphoreType.DMA((N_COPIES,)), pltpu.SemaphoreType.DMA((N_COPIES,)),
    ]
    any_spec = pl.BlockSpec(memory_space=pl.ANY)
    recon, grad_qkv, grad_out, grad_up, grad_down = pl.pallas_call(
        lambda *refs: kernel(sizes, *refs),
        out_shape=(
            jax.ShapeDtypeStruct((4, rows, width), F32),
            jax.ShapeDtypeStruct((3, chunk, local), BF16),
            jax.ShapeDtypeStruct((chunk, local), BF16),
            jax.ShapeDtypeStruct((chunk, hid), BF16),
            jax.ShapeDtypeStruct((chunk, hid), BF16),
        ),
        in_specs=[any_spec] * 7,
        out_specs=(any_spec,) * 5,
        scratch_shapes=scratch,
        compiler_params=pltpu.CompilerParams(
            collective_id=0, has_side_effects=True, vmem_limit_bytes=67043328
        ),
        name="window",
    )(streams[0], head_streams, gains[0], wqkv, wout, w_up[0], w_down[0])
    grad_qkv = jnp.transpose(grad_qkv, (1, 0, 2))
    return (recon[None], grad_qkv[None], grad_out[None], grad_up[None], grad_down[None])


def solution(mesh):
    return jax.shard_map(
        per_device,
        mesh=mesh,
        in_specs=(
            P("section", None, "seq", None),
            P(None, "seq", None),
            P("section", None, None),
            P("section", None, None, "tp"),
            P("section", None, "tp"),
            P("section", None, "tp"),
            P("section", None, "tp"),
        ),
        out_specs=(
            P("section", None, "seq", None),
            P("section", "seq", None, "tp"),
            P("section", "seq", "tp"),
            P("section", "seq", "tp"),
            P("section", "seq", "tp"),
        ),
        check_vma=False,
    )
```

```python
import math

import jax
import jax.numpy as jnp
from jax import lax
from jax.experimental import pallas as pl
from jax.experimental.pallas import tpu as pltpu
from jax.sharding import PartitionSpec as P

MESH = pl.DeviceIdType.MESH
BF16 = jnp.bfloat16
F32 = jnp.float32
HEAD_DIM = 64
PAIR = 2 * HEAD_DIM
N_TP = 4
N_Z = 4
N_SEQ = 8
N_SEC = 4
KV_X_FIRST = 2
DKV_X_FIRST = 3
HIDDEN_X_FIRST = 768
NU, GL, AL, TL = 0, 1, 2, 3
NN = (((1,), (0,)), ((), ()))
NT = (((1,), (1,)), ((), ()))
TN = (((0,), (0,)), ((), ()))


def dot(a, b, dims):
    return lax.dot_general(a, b, dims, preferred_element_type=F32)


def loop(count, size, body):
    def step(i, carry):
        body(pl.multiple_of(i * size, size))
        return carry

    lax.fori_loop(0, count, step, 0)


def unit_of(values):
    centre = values - jnp.mean(values, -1, keepdims=True)
    inv_std = lax.rsqrt(jnp.mean(centre * centre, -1, keepdims=True) + 1e-06)
    return centre * inv_std, inv_std


def norm_back(grad, gain, values):
    unit, inv_std = unit_of(values)
    scaled = grad * gain
    return inv_std * (
        scaled
        - jnp.mean(scaled, -1, keepdims=True)
        - unit * jnp.mean(scaled * unit, -1, keepdims=True)
    )


GELU_C = math.sqrt(2.0 / math.pi)


def gelu(x):
    return 0.5 * x * (1.0 + jnp.tanh(GELU_C * (x + 0.044715 * (x * x * x))))


def gelu_slope(x):
    t = jnp.tanh(GELU_C * (x + 0.044715 * (x * x * x)))
    return 0.5 * (1.0 + t) + 0.5 * x * (1.0 - t * t) * (GELU_C * (1.0 + 0.134145 * (x * x)))


class Sender:
    def __init__(self, send_sem, recv_sem):
        self.send_sem, self.recv_sem = send_sem, recv_sem
        self.all = []

    def start(self, src, dst, device):
        k = len(self.all)
        copy = pltpu.make_async_remote_copy(
            src_ref=src,
            dst_ref=dst,
            send_sem=self.send_sem.at[k],
            recv_sem=self.recv_sem.at[k],
            device_id=device,
            device_id_type=MESH,
        )
        copy.start()
        self.all.append(copy)
        return copy


def received(copies):
    for copy in copies:
        copy.wait_recv()


def kernel(sizes, *refs):
    rows, width, hid, att, cut_mlp, cut_att = sizes
    (streams_h, head_h, gains_h, wqkv_h, wout_h, wup_h, wdn_h) = refs[:7]
    (recon_h, gqkv_h, gout_h, gup_h, gdn_h) = refs[7:12]
    (
        xs, hd, gains, wkv, wqo, wup, wdn,
        rx, sx, fl, gp, hall, glt, gsl, dkvf, dqf, mxf,
        snd, rr, ag, kvb, dks, dax, daz, dbz, dbx, pre, qd, scores, pd,
        gmlp, gatt, gkv, xa_m, pa_m, fa_m, pb_m, fb_m, xb_m, xa_a, pa_a, fa_a, pb_a, fb_a, xb_a,
        xa_k, pa_k, fa_k, pb_k, fb_k, xb_k, om, oqkv, oout,
        load_sem, out_sem, send_sem, recv_sem,
    ) = refs[12:]
    heads = att // PAIR
    sec = lax.axis_index("section")
    seq = lax.axis_index("seq")
    tp = lax.axis_index("tp")
    x_hi, z = seq // N_Z, lax.rem(seq, N_Z)
    quarter = rows // N_TP
    chunk = width // N_SEQ
    half = width // 2
    mine = pl.ds(pl.multiple_of(tp * quarter, quarter), quarter)

    def tp_dev(d):
        return {"tp": lax.rem(tp + d, N_TP)}

    def seq_dev(d):
        return {"seq": lax.rem(x_hi + d // N_Z, 2) * N_Z + lax.rem(z + d % N_Z, N_Z)}

    def seq_back(d):
        return {"seq": lax.rem(x_hi + d // N_Z, 2) * N_Z + lax.rem(z + N_Z - d % N_Z, N_Z)}

    def sec_dev(by, d):
        return {"section": lax.rem(sec + by, N_SEC), "tp": lax.rem(tp + d, N_TP)}

    barrier = pltpu.get_barrier_semaphore()
    for d in range(1, N_TP):
        pl.semaphore_signal(barrier, inc=1, device_id=tp_dev(d), device_id_type=MESH)
    for d in range(1, N_SEQ):
        pl.semaphore_signal(barrier, inc=1, device_id=seq_dev(d), device_id_type=MESH)
    for d in range(N_TP):
        pl.semaphore_signal(barrier, inc=1, device_id=sec_dev(1, d), device_id_type=MESH)

    moves = (
        (gains_h, gains), (streams_h.at[0], xs.at[0]), (wup_h, wup), (wdn_h, wdn),
        (streams_h.at[3], xs.at[3]), (streams_h.at[1], xs.at[1]), (streams_h.at[2], xs.at[2]),
        (wqkv_h.at[1], wkv.at[:, 0]), (wqkv_h.at[2], wkv.at[:, 1]),
        (wqkv_h.at[0], wqo.at[:, 0]), (wout_h, wqo.at[:, 1]), (head_h, hd),
    )
    loads = []

    def load(count):
        for src, dst in moves[len(loads) : len(loads) + count]:
            copy = pltpu.make_async_copy(src, dst, load_sem.at[len(loads)])
            copy.start()
            loads.append(copy)

    load(5)
    sender = Sender(send_sem, recv_sem)

    lane = lax.broadcasted_iota(jnp.int32, (rows, PAIR), 1)
    lane_all = lax.rem(lax.broadcasted_iota(jnp.int32, (rows, att), 1), PAIR)

    def peer_rows(d):
        return pl.ds(pl.multiple_of(lax.rem(tp + d, N_TP) * quarter, quarter), quarter)

    def scatter(t, k):
        return [
            sender.start(snd.at[t, k, peer_rows(d), :], rr.at[t, k, d - 1], tp_dev(d))
            for d in range(1, N_TP)
        ]

    def summed(t, k, copies):
        received(copies)
        total = snd[t, k, mine, :].astype(F32)
        for d in range(N_TP - 1):
            total = total + rr[t, k, d].astype(F32)
        return total

    def spread(slot, value):
        ag[slot, mine, :] = value.astype(BF16)
        return [
            sender.start(ag.at[slot, mine, :], ag.at[slot, mine, :], tp_dev(d)) for d in range(1, N_TP)
        ]

    def send_section(slot, value):
        sx[slot] = value.astype(BF16)
        return [
            sender.start(sx.at[slot], rx.at[slot * 3, mine, :], sec_dev(N_SEC - 1, d))
            for d in range(N_TP)
        ]

    def section_spread(k, copy):
        received([copy])
        return [
            sender.start(rx.at[k, mine, :], rx.at[k, mine, :], tp_dev(d)) for d in range(1, N_TP)
        ]

    def mlp_forward(t, x):
        gain = gains[1:2, :]

        def norm(r):
            unit, _ = unit_of(x[0, pl.ds(r, 32), :])
            fl[NU, pl.ds(t * rows + r, 32), :] = (unit * gain).astype(BF16)

        loop(rows // 32, 32, norm)

    def mlp_hidden(t):
        def up(c):
            out = dot(fl[NU, pl.ds(t * rows, rows), :], wup[:, pl.ds(c, 256)], NN)
            pre[:, pl.ds(c, 256)] = out
            hall[t, 0, 0, :, pl.ds(c, 256)] = gelu(out).astype(BF16)

        loop(hid // 256, 256, up)

    def mlp_down(t):
        def down(c):
            snd[t, 0, :, pl.ds(c, 256)] = dot(
                hall[t, 0, 0], wdn[pl.ds(c, 256), :], NT
            ).astype(BF16)

        loop(width // 256, 256, down)

    def mlp_back(t, x):
        def low(r):
            fl[GL, pl.ds(t * rows + r, 32), :] = x[3, pl.ds(r, 32), :].astype(BF16)

        loop(rows // 32, 32, low)

        def back(c):
            grad = dot(fl[GL, pl.ds(t * rows, rows), :], wdn[:, pl.ds(c, 256)], NN)
            gp[pl.ds(t * rows, rows), pl.ds(c, 256)] = (
                grad * gelu_slope(pre[:, pl.ds(c, 256)])
            ).astype(BF16)

        loop(hid // 256, 256, back)

        def out(c):
            snd[t, 1, :, pl.ds(c, 256)] = dot(
                gp[pl.ds(t * rows, rows), :], wup[pl.ds(c, 256), :], NT
            ).astype(BF16)

        loop(width // 256, 256, out)

    def share(ref, t, cut):
        own, left = ref.at[t, 0, 0], pl.ds(0, cut)
        across = sender.start(own.at[:, left], ref.at[t, 1, 0, :, left], seq_dev(N_Z))
        along = [sender.start(own, ref.at[t, 0, d], seq_dev(d)) for d in (1, 3)]
        return across, along

    def share_rest(ref, t, cut, copies):
        across, along = copies
        own, right = ref.at[t, 0, 0], pl.ds(cut, ref.shape[4] - cut)
        far = sender.start(own, ref.at[t, 0, 2], seq_dev(2))
        rest = sender.start(own.at[:, right], ref.at[t, 1, 0, :, right], seq_dev(N_Z))
        return across, along + [far], rest

    def share_pass(ref, t, cut, copies):
        across, along, rest = copies
        left, right = pl.ds(0, cut), pl.ds(cut, ref.shape[4] - cut)
        received([across])
        late = [
            sender.start(ref.at[t, 1, 0, :, left], ref.at[t, 1, d, :, left], seq_dev(d))
            for d in range(1, N_Z)
        ]
        received(along)
        late += [
            sender.start(ref.at[t, 0, d, :, right], ref.at[t, 1, d, :, right], seq_dev(N_Z))
            for d in range(1, N_Z)
        ]
        return late + [rest]

    def slices_out(t, factor, turned, gathered):
        def turn(c):
            tile = fl[factor, pl.ds(t * rows, rows), pl.ds(c, 128)]
            turned[t, pl.ds(c, 128), :] = tile.astype(F32).T.astype(BF16)

        loop(width // 128, 128, turn)
        gathered[:, pl.ds(t * N_SEQ * rows, rows)] = turned[t, grad_rows(0, 0), :]

    def slices_send(t, turned, gathered):
        return [
            sender.start(
                turned.at[t, grad_rows(d // N_Z, d % N_Z), :],
                gathered.at[:, pl.ds((t * N_SEQ + d) * rows, rows)],
                seq_dev(d),
            )
            for d in range(1, N_SEQ)
        ]

    def grads_down(copies):
        received(copies)

        def tile(c):
            cols = pl.ds(c, 256)
            om[1, :, cols] = dot(
                gsl[...], hall[:, :, :, :, cols].reshape(2 * N_SEQ * rows, 256), NN
            ).astype(BF16)

        loop(hid // 256, 256, tile)

    def attention_in(t, x, slot):
        gain = gains[0:1, :]

        def low(r):
            value = x[1, pl.ds(r, 32), :] - ag[slot, pl.ds(r, 32), :].astype(F32)
            x[1, pl.ds(r, 32), :] = value
            if t == 0:
                rx_low[pl.ds(r, 32), :] = value.astype(BF16)
            unit, _ = unit_of(value)
            fl[AL, pl.ds(t * rows + r, 32), :] = (unit * gain).astype(BF16)

        rx_low = snd.at[0, 0]
        loop(rows // 32, 32, low)
        packed = dot(fl[AL, pl.ds(t * rows, rows), :], wkv[...].reshape(att, width), NT).astype(BF16)
        across, along = [], []
        for h in range(heads):
            kvb[t, h, 0, 0] = packed[:, h * PAIR : (h + 1) * PAIR]
            across.append(sender.start(kvb.at[t, h, 0, 0], kvb.at[t, h, 1, 0], seq_dev(N_Z)))
            along.append(
                [sender.start(kvb.at[t, h, 0, 0], kvb.at[t, h, 0, d], seq_dev(d)) for d in range(1, N_Z)]
            )
        query = dot(fl[AL, pl.ds(t * rows, rows), :], wqo[...].reshape(att, width), NT)
        query = query.astype(BF16).astype(F32) * 0.125
        qd[pl.ds(0, rows), :] = jnp.where(lane_all < HEAD_DIM, query, 0.0).astype(BF16)
        return across, along

    def pass_along(t, copies):
        across, along = copies
        late = []
        for h in range(KV_X_FIRST):
            received([across[h]])
            late.append(
                [sender.start(kvb.at[t, h, 1, 0], kvb.at[t, h, 1, d], seq_dev(d)) for d in range(1, N_Z)]
            )
        return late

    def pass_across(t, copies, late):
        across, along = copies
        for h in range(KV_X_FIRST, heads):
            received(along[h])
            late.append(
                [sender.start(kvb.at[t, h, 0, d], kvb.at[t, h, 1, d], seq_dev(N_Z)) for d in range(1, N_Z)]
            )
        return late

    def grads_in(t, x, slot):
        gain = gains[1:2, :]

        def total(r):
            grad = ag[slot, pl.ds(r, 32), :].astype(F32)
            value = x[2, pl.ds(r, 32), :] + norm_back(grad, gain, x[0, pl.ds(r, 32), :])
            x[2, pl.ds(r, 32), :] = value
            fl[TL, pl.ds(t * rows + r, 32), :] = value.astype(BF16)

        loop(rows // 32, 32, total)
        grad = dot(fl[TL, pl.ds(t * rows, rows), :], wqo[...].reshape(att, width), NT)
        qd[pl.ds(rows, rows), :] = jnp.where(lane_all >= HEAD_DIM, grad, 0.0).astype(BF16)

    def attend(t, copies, late):
        across, along = copies
        tokens = N_SEQ * rows
        first = []
        for h in range(heads):
            lanes = pl.ds(h * PAIR, PAIR)
            if h < KV_X_FIRST:
                received(along[h])
            else:
                received([across[h]])
            received(late[h])
            kv = kvb[t, h].reshape(tokens, PAIR)
            both = qd[:, lanes]
            scores[...] = dot(kv, both, NT)
            logits = scores[:, :rows]
            weight = jnp.exp(logits - jnp.max(logits, 0, keepdims=True))
            probs = weight * (1.0 / jnp.sum(weight, 0, keepdims=True))
            grad_probs = scores[:, rows:]
            delta = jnp.sum(probs * grad_probs, 0, keepdims=True)
            pd[:, rows:] = probs.astype(BF16)
            pd[:, :rows] = (probs * (grad_probs - delta)).astype(BF16)
            dks[t, h] = dot(pd[...], both, NN).astype(BF16).reshape(2, N_Z, rows, PAIR)
            if h < DKV_X_FIRST:
                first.append([sender.start(dks.at[t, h, 1], dax.at[t, h], seq_dev(N_Z))])
            else:
                first.append(
                    [
                        sender.start(dks.at[t, h, :, d], dbz.at[t, h - DKV_X_FIRST, d - 1], seq_back(d))
                        for d in range(1, N_Z)
                    ]
                )
            mixed = dot(kv, pd[...], TN).T
            dqf[pl.ds(t * rows, rows), lanes] = jnp.where(lane < HEAD_DIM, mixed[:rows] * 0.125, 0.0).astype(BF16)
            mxf[pl.ds(t * rows, rows), lanes] = jnp.where(lane >= HEAD_DIM, mixed[rows:], 0.0).astype(BF16)
        return first

    def attention_out(t):
        def out(c):
            snd[t, 2, :, pl.ds(c, 256)] = dot(
                mxf[pl.ds(t * rows, rows), :], wqo[:, :, :, pl.ds(c, 256)].reshape(att, 256), NN
            ).astype(BF16)

        loop(width // 256, 256, out)
        return scatter(t, 2)

    def attention_relay(t, first):
        last = []
        for h in range(heads):
            received(first[h])
            if h < DKV_X_FIRST:
                for d in (1, 2, 3, 0):
                    dks[t, h, 0, d] = (
                        dks[t, h, 0, d].astype(F32) + dax[t, h, d].astype(F32)
                    ).astype(BF16)
                    if d > 0:
                        last.append(sender.start(dks.at[t, h, 0, d], daz.at[t, h, d - 1], seq_back(d)))
            else:
                k = h - DKV_X_FIRST
                for side in (1, 0):
                    total = dks[t, h, side, 0].astype(F32)
                    for d in range(N_Z - 1):
                        total = total + dbz[t, k, d, side].astype(F32)
                    dks[t, h, side, 0] = total.astype(BF16)
                last.append(sender.start(dks.at[t, h, 1, 0], dbx.at[t, k], seq_dev(N_Z)))
        return last

    def attention_back(t, last):
        received(last)
        for h in range(heads):
            total = dks[t, h, 0, 0].astype(F32)
            if h < DKV_X_FIRST:
                for d in range(N_Z - 1):
                    total = total + daz[t, h, d].astype(F32)
            else:
                total = total + dbx[t, h - DKV_X_FIRST].astype(F32)
            dkvf[pl.ds(t * rows, rows), pl.ds(h * PAIR, PAIR)] = total.astype(BF16)

        def out(c):
            cols = pl.ds(c, 256)
            snd[t, 3, :, cols] = (
                dot(dkvf[pl.ds(t * rows, rows), :], wkv[:, :, :, cols].reshape(att, 256), NN)
                + dot(dqf[pl.ds(t * rows, rows), :], wqo[:, :, :, cols].reshape(att, 256), NN)
            ).astype(BF16)

        loop(width // 256, 256, out)
        return scatter(t, 3)

    def grad_rows(by_x, by_z):
        index = lax.rem(x_hi + by_x, 2) * N_Z + lax.rem(z + by_z, N_Z)
        return pl.ds(pl.multiple_of(index * chunk, 32), chunk)

    part = chunk // 2

    def part_rows(by_x, by_z, side):
        index = lax.rem(x_hi + by_x, 2) * N_Z + lax.rem(z + by_z, N_Z)
        return index * chunk + side * part

    def add_rows(g, cols, start, count, *terms):
        def add(r):
            here = pl.ds(pl.multiple_of(start + r, 16), 16)
            total = g[here, cols].astype(F32)
            for term in terms:
                total = total + term(pl.ds(r, 16)).astype(F32)
            g[here, cols] = total.astype(BF16)

        loop(count // 16, 16, add)

    def ring_start(g, cols, ks, pass_buf, final):
        def ship(k, d, side, dst, to):
            rows_at = pl.ds(pl.multiple_of(part_rows(k, d, side), 16), part)
            return sender.start(g.at[rows_at, cols], dst, seq_dev(to))

        up = [ship(k, 2, 0, pass_buf.at[0, i], 1) for i, k in enumerate(ks)]
        down = [ship(k, 2, 1, pass_buf.at[1, i], 3) for i, k in enumerate(ks)]
        rest = []
        for i, k in enumerate(ks):
            rest.append(ship(k, 1, 1, final.at[0, i, pl.ds(part, part)], 1))
            rest.append(ship(k, 3, 0, final.at[1, i, pl.ds(0, part)], 3))
        return up, down, rest

    def ring_relay(g, cols, ks, pass_buf, final, copies):
        up, down, rest = copies
        for i, k in enumerate(ks):
            for group, d, side in ((up, 1, 0), (down, 3, 1)):
                received([group[i]])
                start = part_rows(k, d, side)
                add_rows(g, cols, start, part, lambda here, side=side: pass_buf[side, i, here, :])
                rows_at = pl.ds(pl.multiple_of(start, 16), part)
                rest.append(
                    sender.start(g.at[rows_at, cols], final.at[side, i, pl.ds(side * part, part)], seq_dev(d))
                )
        return rest

    class Reduction:
        def __init__(self, g, cut, xa, pa, fa, pb, fb, xb):
            self.g, self.xa, self.pa, self.fa, self.pb, self.fb, self.xb = g, xa, pa, fa, pb, fb, xb
            self.cols_a, self.cols_b = pl.ds(0, cut), pl.ds(cut, g.shape[1] - cut)

        def first(self):
            other = pl.ds(pl.multiple_of((1 - x_hi) * half, 32), half)
            self.across = [sender.start(self.g.at[other, self.cols_a], self.xa, seq_dev(N_Z))]
            self.ring_b = ring_start(self.g, self.cols_b, (1, 0), self.pb, self.fb)

        def second_b(self):
            self.rest_b = ring_relay(self.g, self.cols_b, (1, 0), self.pb, self.fb, self.ring_b)

        def second_a(self):
            received(self.across)
            add_rows(self.g, self.cols_a, x_hi * half, half, lambda here: self.xa[here, :])
            self.ring_a = ring_start(self.g, self.cols_a, (0,), self.pa, self.fa)

        def third(self):
            self.rest_a = ring_relay(self.g, self.cols_a, (0,), self.pa, self.fa, self.ring_a)
            received(self.rest_b)
            for i, k in enumerate((1, 0)):
                add_rows(
                    self.g, self.cols_b, part_rows(k, 0, 0), chunk,
                    lambda here, i=i: self.fb[0, i, here, :], lambda here, i=i: self.fb[1, i, here, :],
                )
                if k == 1:
                    rows_at = pl.ds(pl.multiple_of(part_rows(1, 0, 0), 16), chunk)
                    self.back = [sender.start(self.g.at[rows_at, self.cols_b], self.xb, seq_dev(N_Z))]

        def last(self, store):
            received(self.rest_a)
            received(self.back)
            start = seq * chunk

            def add(r):
                here, out = pl.ds(pl.multiple_of(start + r, 32), 32), pl.ds(r, 32)
                left = self.g[here, self.cols_a].astype(F32)
                for k in range(2):
                    left = left + self.fa[k, 0, out, :].astype(F32)
                right = self.g[here, self.cols_b].astype(F32) + self.xb[out, :].astype(F32)
                store(out, left.astype(BF16), right.astype(BF16))

            loop(chunk // 32, 32, add)

    red_m = Reduction(gmlp, cut_mlp, xa_m, pa_m, fa_m, pb_m, fb_m, xb_m)
    red_a = Reduction(gatt, cut_att, xa_a, pa_a, fa_a, pb_a, fb_a, xb_a)
    red_k = Reduction(gkv, cut_att, xa_k, pa_k, fa_k, pb_k, fb_k, xb_k)

    def store_mlp(here, left, right):
        om[0, here, pl.ds(0, cut_mlp)] = left
        om[0, here, pl.ds(cut_mlp, hid - cut_mlp)] = right

    def joined(left, right, k):
        pieces = []
        for h in range(heads):
            start = h * PAIR + k * HEAD_DIM
            if start < cut_att:
                pieces.append(left[:, start : start + HEAD_DIM])
            else:
                pieces.append(right[:, start - cut_att : start - cut_att + HEAD_DIM])
        return jnp.concatenate(pieces, 1)

    def store_qo(here, left, right):
        oqkv[0, here, :] = joined(left, right, 0)
        oout[here, :] = joined(left, right, 1)

    def store_kv(here, left, right):
        oqkv[1, here, :] = joined(left, right, 0)
        oqkv[2, here, :] = joined(left, right, 1)

    def grads_mlp():
        def tile(c):
            gmlp[pl.ds(c, 256), :] = dot(fl[NU, :, pl.ds(c, 256)], gp[...], TN).astype(BF16)

        loop(width // 256, 256, tile)

    def grads_att():
        def tile(c):
            gatt[pl.ds(c, 256), :] = (
                dot(fl[AL, :, pl.ds(c, 256)], dqf[...], TN) + dot(fl[TL, :, pl.ds(c, 256)], mxf[...], TN)
            ).astype(BF16)

        loop(width // 256, 256, tile)
        red_a.first()

    def grads_kv():
        def tile(c):
            gkv[pl.ds(c, 256), :] = dot(fl[AL, :, pl.ds(c, 256)], dkvf[...], TN).astype(BF16)

        loop(width // 256, 256, tile)
        red_k.first()

    loads[0].wait()
    loads[1].wait()
    mlp_forward(0, xs)
    loads[2].wait()
    mlp_hidden(0)
    loads[3].wait()
    load(7)
    mlp_down(0)
    pl.semaphore_wait(barrier, N_TP - 1 + N_SEQ - 1 + N_TP)
    c_mlp = c_first = scatter(0, 0)
    c_hid = share(hall, 0, HIDDEN_X_FIRST)
    loads[4].wait()
    mlp_back(0, xs)
    slices_out(0, GL, glt, gsl)
    c_mlp = spread(0, summed(0, 0, c_mlp))
    received(c_mlp)
    c_grad = scatter(0, 1)
    for k in range(5, 11):
        loads[k].wait()
    for copy in c_first:
        copy.wait_send()
    c_kv = attention_in(0, xs, 0)
    c_low = sender.start(snd.at[0, 0, mine, :], rx.at[1, mine, :], sec_dev(N_SEC - 1, 0))
    late = pass_along(0, c_kv)
    c_grad = spread(1, summed(0, 1, c_grad))
    late = pass_across(0, c_kv, late)
    c_down = slices_send(0, glt, gsl)
    c_hid = share_rest(hall, 0, HIDDEN_X_FIRST, c_hid)
    received(c_grad)
    grads_in(0, xs, 1)
    c_total = sender.start(
        fl.at[TL, mine, :], rx.at[2, mine, :], sec_dev(N_SEC - 1, 0)
    )
    c_low = section_spread(1, c_low)
    c_dkv = attend(0, c_kv, late)
    c_att = attention_out(0)
    c_dkv = attention_relay(0, c_dkv)
    c_up = send_section(0, xs[0, mine, :] - summed(0, 2, c_att))
    c_down += share_pass(hall, 0, HIDDEN_X_FIRST, c_hid)

    is_last = sec == N_SEC - 1
    loads[11].wait()

    def choose(k):
        def one(r):
            hd[k, pl.ds(r, 32), :] = jnp.where(
                is_last, hd[k, pl.ds(r, 32), :], rx[k, pl.ds(r, 32), :].astype(F32)
            )

        loop(rows // 32, 32, one)

    outs = []

    def emit(k):
        copy = pltpu.make_async_copy(hd.at[k], recon_h.at[k], out_sem.at[k])
        copy.start()
        outs.append(copy)

    def finish(src, dst, k):
        copy = pltpu.make_async_copy(src, dst, out_sem.at[k])
        copy.start()
        outs.append(copy)

    slope = gains[0:1, :]
    c_att = attention_back(0, c_dkv)
    received(c_up)
    choose(0)
    mlp_forward(1, hd)
    mlp_hidden(1)
    mlp_down(1)
    c_mlp = scatter(1, 0)
    c_hid = share_rest(hall, 1, HIDDEN_X_FIRST, share(hall, 1, HIDDEN_X_FIRST))
    grad = summed(0, 3, c_att)
    c_gl = send_section(1, xs[3, mine, :] + norm_back(grad, slope, xs[1, mine, :]))
    c_mlp = spread(2, summed(1, 0, c_mlp))
    received(c_low)
    choose(1)
    received(c_gl)
    choose(3)
    mlp_back(1, hd)
    c_grad = scatter(1, 1)
    received(c_mlp)
    c_kv = attention_in(1, hd, 2)
    emit(1)
    c_total = section_spread(2, c_total)
    grads_mlp()
    c_grad = spread(3, summed(1, 1, c_grad))
    late = pass_along(1, c_kv)
    slices_out(1, GL, glt, gsl)
    late = pass_across(1, c_kv, late)
    red_m.first()
    received(c_total)
    choose(2)
    received(c_grad)
    grads_in(1, hd, 3)
    emit(2)
    c_dkv = attend(1, c_kv, late)
    c_att = attention_out(1)
    red_m.second_b()
    c_down += share_pass(hall, 1, HIDDEN_X_FIRST, c_hid)
    c_dkv = attention_relay(1, c_dkv)
    red_m.second_a()
    grads_att()
    c_up = spread(4, summed(1, 2, c_att))
    c_att = attention_back(1, c_dkv)
    grads_kv()
    c_down += slices_send(1, glt, gsl)
    c_gl = spread(5, summed(1, 3, c_att))
    red_m.third()
    received(c_up)

    def upper(r):
        here = pl.ds(r, 32)
        value = hd[0, here, :]
        pre[here, :] = value - ag[4, here, :].astype(F32)

    loop(rows // 32, 32, upper)
    copy = pltpu.make_async_copy(pre, recon_h.at[0], out_sem.at[0])
    copy.start()
    outs.append(copy)
    red_a.second_b()
    red_a.second_a()
    received(c_gl)

    def lower(r):
        here = pl.ds(r, 32)
        hd[3, here, :] = hd[3, here, :] + norm_back(ag[5, here, :].astype(F32), slope, hd[1, here, :])

    loop(rows // 32, 32, lower)
    emit(3)
    red_k.second_b()
    red_k.second_a()
    red_a.third()
    grads_down(c_down)
    finish(om.at[1], gdn_h, 5)
    red_m.last(store_mlp)
    finish(om.at[0], gup_h, 4)
    red_k.third()
    red_a.last(store_qo)
    finish(oout, gout_h, 7)
    red_k.last(store_kv)
    finish(oqkv, gqkv_h, 6)
    for copy in [c for c in sender.all if all(c is not f for f in c_first)]:
        copy.wait_send()
    for copy in outs:
        copy.wait()


N_COPIES = 320


def per_device(streams, head_streams, gains, w_qkv, w_out, w_up, w_down):
    rows, width = streams.shape[2], streams.shape[3]
    hid = w_up.shape[2]
    local = w_out.shape[2]
    att = 2 * local
    heads = local // HEAD_DIM
    chunk = width // N_SEQ
    half = width // 2
    cut_mlp = 512
    cut_att = 256
    wqkv = jnp.transpose(w_qkv[0], (1, 2, 0)).reshape(3, heads, HEAD_DIM, width)
    wout = jnp.transpose(w_out[0], (1, 0)).reshape(heads, HEAD_DIM, width)
    sizes = (rows, width, hid, att, cut_mlp, cut_att)
    quarter = rows // N_TP
    rest_m, rest_a = hid - cut_mlp, att - cut_att
    n_dx, n_dz = DKV_X_FIRST, heads - DKV_X_FIRST
    vm = pltpu.VMEM

    def ring_buffers(left, right):
        return (
            vm((half, left), BF16), vm((2, 1, chunk // 2, left), BF16), vm((2, 1, chunk, left), BF16),
            vm((2, 2, chunk // 2, right), BF16), vm((2, 2, chunk, right), BF16), vm((chunk, right), BF16),
        )

    scratch = [
        vm((4, rows, width), F32), vm((4, rows, width), F32), vm((2, width), F32),
        vm((heads, 2, HEAD_DIM, width), BF16), vm((heads, 2, HEAD_DIM, width), BF16),
        vm((width, hid), BF16), vm((width, hid), BF16),
        vm((4, rows, width), BF16), vm((2, quarter, width), BF16),
        vm((4, 2 * rows, width), BF16), vm((2 * rows, hid), BF16),
        vm((2, 2, N_Z, rows, hid), BF16), vm((2, width, rows), BF16), vm((chunk, 2 * N_SEQ * rows), BF16),
        vm((2 * rows, att), BF16), vm((2 * rows, att), BF16), vm((2 * rows, att), BF16),
        vm((2, 4, rows, width), BF16), vm((2, 4, N_TP - 1, quarter, width), BF16), vm((6, rows, width), BF16),
        vm((2, heads, 2, N_Z, rows, PAIR), BF16), vm((2, heads, 2, N_Z, rows, PAIR), BF16),
        vm((2, n_dx, N_Z, rows, PAIR), BF16), vm((2, n_dx, N_Z - 1, rows, PAIR), BF16),
        vm((2, n_dz, N_Z - 1, 2, rows, PAIR), BF16), vm((2, n_dz, rows, PAIR), BF16),
        vm((rows, hid), F32), vm((2 * rows, att), BF16),
        vm((N_SEQ * rows, 2 * rows), F32), vm((N_SEQ * rows, 2 * rows), BF16),
        vm((width, hid), BF16), vm((width, att), BF16), vm((width, att), BF16),
        *ring_buffers(cut_mlp, rest_m), *ring_buffers(cut_att, rest_a), *ring_buffers(cut_att, rest_a),
        vm((2, chunk, hid), BF16), vm((3, chunk, local), BF16), vm((chunk, local), BF16),
        pltpu.SemaphoreType.DMA((12,)), pltpu.SemaphoreType.DMA((8,)),
        pltpu.SemaphoreType.DMA((N_COPIES,)), pltpu.SemaphoreType.DMA((N_COPIES,)),
    ]
    any_spec = pl.BlockSpec(memory_space=pl.ANY)
    recon, grad_qkv, grad_out, grad_up, grad_down = pl.pallas_call(
        lambda *refs: kernel(sizes, *refs),
        out_shape=(
            jax.ShapeDtypeStruct((4, rows, width), F32),
            jax.ShapeDtypeStruct((3, chunk, local), BF16),
            jax.ShapeDtypeStruct((chunk, local), BF16),
            jax.ShapeDtypeStruct((chunk, hid), BF16),
            jax.ShapeDtypeStruct((chunk, hid), BF16),
        ),
        in_specs=[any_spec] * 7,
        out_specs=(any_spec,) * 5,
        scratch_shapes=scratch,
        compiler_params=pltpu.CompilerParams(
            collective_id=0, has_side_effects=True, vmem_limit_bytes=67043328
        ),
        name="window",
    )(streams[0], head_streams, gains[0], wqkv, wout, w_up[0], w_down[0])
    grad_qkv = jnp.transpose(grad_qkv, (1, 0, 2))
    return (recon[None], grad_qkv[None], grad_out[None], grad_up[None], grad_down[None])


def solution(mesh):
    return jax.shard_map(
        per_device,
        mesh=mesh,
        in_specs=(
            P("section", None, "seq", None),
            P(None, "seq", None),
            P("section", None, None),
            P("section", None, None, "tp"),
            P("section", None, "tp"),
            P("section", None, "tp"),
            P("section", None, "tp"),
        ),
        out_specs=(
            P("section", None, "seq", None),
            P("section", "seq", None, "tp"),
            P("section", "seq", "tp"),
            P("section", "seq", "tp"),
            P("section", "seq", "tp"),
        ),
        check_vma=False,
    )
```

```python
import math

import jax
import jax.numpy as jnp
from jax import lax
from jax.experimental import pallas as pl
from jax.experimental.pallas import tpu as pltpu
from jax.sharding import PartitionSpec as P

MESH = pl.DeviceIdType.MESH
BF16 = jnp.bfloat16
F32 = jnp.float32
HEAD_DIM = 64
PAIR = 2 * HEAD_DIM
N_TP = 4
N_Z = 4
N_SEQ = 8
N_SEC = 4
KV_X_FIRST = 2
DKV_X_FIRST = 3
HIDDEN_X_FIRST = 1024
NU, GL, AL, TL = 0, 1, 2, 3
NN = (((1,), (0,)), ((), ()))
NT = (((1,), (1,)), ((), ()))
TN = (((0,), (0,)), ((), ()))


def dot(a, b, dims):
    return lax.dot_general(a, b, dims, preferred_element_type=F32)


def loop(count, size, body):
    def step(i, carry):
        body(pl.multiple_of(i * size, size))
        return carry

    lax.fori_loop(0, count, step, 0)


def unit_of(values):
    centre = values - jnp.mean(values, -1, keepdims=True)
    inv_std = lax.rsqrt(jnp.mean(centre * centre, -1, keepdims=True) + 1e-06)
    return centre * inv_std, inv_std


def norm_back(grad, gain, values):
    unit, inv_std = unit_of(values)
    scaled = grad * gain
    return inv_std * (
        scaled
        - jnp.mean(scaled, -1, keepdims=True)
        - unit * jnp.mean(scaled * unit, -1, keepdims=True)
    )


GELU_C = math.sqrt(2.0 / math.pi)


def gelu(x):
    return 0.5 * x * (1.0 + jnp.tanh(GELU_C * (x + 0.044715 * (x * x * x))))


def gelu_slope(x):
    t = jnp.tanh(GELU_C * (x + 0.044715 * (x * x * x)))
    return 0.5 * (1.0 + t) + 0.5 * x * (1.0 - t * t) * (GELU_C * (1.0 + 0.134145 * (x * x)))


class Sender:
    def __init__(self, send_sem, recv_sem):
        self.send_sem, self.recv_sem = send_sem, recv_sem
        self.all = []

    def start(self, src, dst, device):
        k = len(self.all)
        copy = pltpu.make_async_remote_copy(
            src_ref=src,
            dst_ref=dst,
            send_sem=self.send_sem.at[k],
            recv_sem=self.recv_sem.at[k],
            device_id=device,
            device_id_type=MESH,
        )
        copy.start()
        self.all.append(copy)
        return copy


def received(copies):
    for copy in copies:
        copy.wait_recv()


def kernel(sizes, *refs):
    rows, width, hid, att, cut_mlp, cut_att = sizes
    (streams_h, head_h, gains_h, wqkv_h, wout_h, wup_h, wdn_h) = refs[:7]
    (recon_h, gqkv_h, gout_h, gup_h, gdn_h) = refs[7:12]
    (
        xs, hd, gains, wkv, wqo, wup, wdn,
        rx, sx, fl, gp, hall, glt, gsl, dkvf, dqf, mxf,
        snd, rr, ag, kvb, dks, dax, daz, dbz, dbx, pre, qd, scores, pd,
        gmlp, gatt, gkv, xa_m, pa_m, fa_m, pb_m, fb_m, xb_m, xa_a, pa_a, fa_a, pb_a, fb_a, xb_a,
        xa_k, pa_k, fa_k, pb_k, fb_k, xb_k, om, oqkv, oout,
        load_sem, out_sem, send_sem, recv_sem,
    ) = refs[12:]
    heads = att // PAIR
    sec = lax.axis_index("section")
    seq = lax.axis_index("seq")
    tp = lax.axis_index("tp")
    x_hi, z = seq // N_Z, lax.rem(seq, N_Z)
    quarter = rows // N_TP
    chunk = width // N_SEQ
    half = width // 2
    mine = pl.ds(pl.multiple_of(tp * quarter, quarter), quarter)

    def tp_dev(d):
        return {"tp": lax.rem(tp + d, N_TP)}

    def seq_dev(d):
        return {"seq": lax.rem(x_hi + d // N_Z, 2) * N_Z + lax.rem(z + d % N_Z, N_Z)}

    def seq_back(d):
        return {"seq": lax.rem(x_hi + d // N_Z, 2) * N_Z + lax.rem(z + N_Z - d % N_Z, N_Z)}

    def sec_dev(by, d):
        return {"section": lax.rem(sec + by, N_SEC), "tp": lax.rem(tp + d, N_TP)}

    barrier = pltpu.get_barrier_semaphore()
    for d in range(1, N_TP):
        pl.semaphore_signal(barrier, inc=1, device_id=tp_dev(d), device_id_type=MESH)
    for d in range(1, N_SEQ):
        pl.semaphore_signal(barrier, inc=1, device_id=seq_dev(d), device_id_type=MESH)
    for d in range(N_TP):
        pl.semaphore_signal(barrier, inc=1, device_id=sec_dev(1, d), device_id_type=MESH)

    moves = (
        (gains_h, gains), (streams_h.at[0], xs.at[0]), (wup_h, wup), (wdn_h, wdn),
        (streams_h.at[3], xs.at[3]), (streams_h.at[1], xs.at[1]), (streams_h.at[2], xs.at[2]),
        (wqkv_h.at[1], wkv.at[:, 0]), (wqkv_h.at[2], wkv.at[:, 1]),
        (wqkv_h.at[0], wqo.at[:, 0]), (wout_h, wqo.at[:, 1]), (head_h, hd),
    )
    loads = []

    def load(count):
        for src, dst in moves[len(loads) : len(loads) + count]:
            copy = pltpu.make_async_copy(src, dst, load_sem.at[len(loads)])
            copy.start()
            loads.append(copy)

    load(5)
    sender = Sender(send_sem, recv_sem)

    lane = lax.broadcasted_iota(jnp.int32, (rows, PAIR), 1)
    lane_all = lax.rem(lax.broadcasted_iota(jnp.int32, (rows, att), 1), PAIR)

    def peer_rows(d):
        return pl.ds(pl.multiple_of(lax.rem(tp + d, N_TP) * quarter, quarter), quarter)

    def scatter(t, k):
        return [
            sender.start(snd.at[t, k, peer_rows(d), :], rr.at[t, k, d - 1], tp_dev(d))
            for d in range(1, N_TP)
        ]

    def summed(t, k, copies):
        received(copies)
        total = snd[t, k, mine, :].astype(F32)
        for d in range(N_TP - 1):
            total = total + rr[t, k, d].astype(F32)
        return total

    def spread(slot, value):
        ag[slot, mine, :] = value.astype(BF16)
        return [
            sender.start(ag.at[slot, mine, :], ag.at[slot, mine, :], tp_dev(d)) for d in range(1, N_TP)
        ]

    def send_section(slot, value):
        sx[slot] = value.astype(BF16)
        return [
            sender.start(sx.at[slot], rx.at[slot * 3, mine, :], sec_dev(N_SEC - 1, d))
            for d in range(N_TP)
        ]

    def section_spread(k, copy):
        received([copy])
        return [
            sender.start(rx.at[k, mine, :], rx.at[k, mine, :], tp_dev(d)) for d in range(1, N_TP)
        ]

    def mlp_forward(t, x):
        gain = gains[1:2, :]

        def norm(r):
            unit, _ = unit_of(x[0, pl.ds(r, 32), :])
            fl[NU, pl.ds(t * rows + r, 32), :] = (unit * gain).astype(BF16)

        loop(rows // 32, 32, norm)

    def mlp_hidden(t):
        def up(c):
            out = dot(fl[NU, pl.ds(t * rows, rows), :], wup[:, pl.ds(c, 256)], NN)
            pre[:, pl.ds(c, 256)] = out
            hall[t, 0, 0, :, pl.ds(c, 256)] = gelu(out).astype(BF16)

        loop(hid // 256, 256, up)

    def mlp_down(t):
        def down(c):
            snd[t, 0, :, pl.ds(c, 256)] = dot(
                hall[t, 0, 0], wdn[pl.ds(c, 256), :], NT
            ).astype(BF16)

        loop(width // 256, 256, down)

    def mlp_back(t, x):
        def low(r):
            fl[GL, pl.ds(t * rows + r, 32), :] = x[3, pl.ds(r, 32), :].astype(BF16)

        loop(rows // 32, 32, low)

        def back(c):
            grad = dot(fl[GL, pl.ds(t * rows, rows), :], wdn[:, pl.ds(c, 256)], NN)
            gp[pl.ds(t * rows, rows), pl.ds(c, 256)] = (
                grad * gelu_slope(pre[:, pl.ds(c, 256)])
            ).astype(BF16)

        loop(hid // 256, 256, back)

        def out(c):
            snd[t, 1, :, pl.ds(c, 256)] = dot(
                gp[pl.ds(t * rows, rows), :], wup[pl.ds(c, 256), :], NT
            ).astype(BF16)

        loop(width // 256, 256, out)

    def share(ref, t, cut):
        own, left = ref.at[t, 0, 0], pl.ds(0, cut)
        across = sender.start(own.at[:, left], ref.at[t, 1, 0, :, left], seq_dev(N_Z))
        along = [sender.start(own, ref.at[t, 0, d], seq_dev(d)) for d in (1, 3)]
        return across, along

    def share_rest(ref, t, cut, copies):
        across, along = copies
        own, right = ref.at[t, 0, 0], pl.ds(cut, ref.shape[4] - cut)
        far = sender.start(own, ref.at[t, 0, 2], seq_dev(2))
        rest = sender.start(own.at[:, right], ref.at[t, 1, 0, :, right], seq_dev(N_Z))
        return across, along + [far], rest

    def share_pass(ref, t, cut, copies):
        across, along, rest = copies
        left, right = pl.ds(0, cut), pl.ds(cut, ref.shape[4] - cut)
        received([across])
        late = [
            sender.start(ref.at[t, 1, 0, :, left], ref.at[t, 1, d, :, left], seq_dev(d))
            for d in range(1, N_Z)
        ]
        received(along)
        late += [
            sender.start(ref.at[t, 0, d, :, right], ref.at[t, 1, d, :, right], seq_dev(N_Z))
            for d in range(1, N_Z)
        ]
        return late + [rest]

    def slices_out(t, factor, turned, gathered):
        def turn(c):
            tile = fl[factor, pl.ds(t * rows, rows), pl.ds(c, 128)]
            turned[t, pl.ds(c, 128), :] = tile.astype(F32).T.astype(BF16)

        loop(width // 128, 128, turn)
        gathered[:, pl.ds(t * N_SEQ * rows, rows)] = turned[t, grad_rows(0, 0), :]

    def slices_send(t, turned, gathered):
        return [
            sender.start(
                turned.at[t, grad_rows(d // N_Z, d % N_Z), :],
                gathered.at[:, pl.ds((t * N_SEQ + d) * rows, rows)],
                seq_dev(d),
            )
            for d in range(1, N_SEQ)
        ]

    def grads_down(copies):
        received(copies)

        def tile(c):
            cols = pl.ds(c, 256)
            om[1, :, cols] = dot(
                gsl[...], hall[:, :, :, :, cols].reshape(2 * N_SEQ * rows, 256), NN
            ).astype(BF16)

        loop(hid // 256, 256, tile)

    def attention_in(t, x, slot):
        gain = gains[0:1, :]

        def low(r):
            value = x[1, pl.ds(r, 32), :] - ag[slot, pl.ds(r, 32), :].astype(F32)
            x[1, pl.ds(r, 32), :] = value
            if t == 0:
                rx_low[pl.ds(r, 32), :] = value.astype(BF16)
            unit, _ = unit_of(value)
            fl[AL, pl.ds(t * rows + r, 32), :] = (unit * gain).astype(BF16)

        rx_low = snd.at[0, 0]
        loop(rows // 32, 32, low)
        packed = dot(fl[AL, pl.ds(t * rows, rows), :], wkv[...].reshape(att, width), NT).astype(BF16)
        across, along = [], []
        for h in range(heads):
            kvb[t, h, 0, 0] = packed[:, h * PAIR : (h + 1) * PAIR]
            across.append(sender.start(kvb.at[t, h, 0, 0], kvb.at[t, h, 1, 0], seq_dev(N_Z)))
            along.append(
                [sender.start(kvb.at[t, h, 0, 0], kvb.at[t, h, 0, d], seq_dev(d)) for d in range(1, N_Z)]
            )
        query = dot(fl[AL, pl.ds(t * rows, rows), :], wqo[...].reshape(att, width), NT)
        query = query.astype(BF16).astype(F32) * 0.125
        qd[pl.ds(0, rows), :] = jnp.where(lane_all < HEAD_DIM, query, 0.0).astype(BF16)
        return across, along

    def pass_along(t, copies):
        across, along = copies
        late = []
        for h in range(KV_X_FIRST):
            received([across[h]])
            late.append(
                [sender.start(kvb.at[t, h, 1, 0], kvb.at[t, h, 1, d], seq_dev(d)) for d in range(1, N_Z)]
            )
        return late

    def pass_across(t, copies, late):
        across, along = copies
        for h in range(KV_X_FIRST, heads):
            received(along[h])
            late.append(
                [sender.start(kvb.at[t, h, 0, d], kvb.at[t, h, 1, d], seq_dev(N_Z)) for d in range(1, N_Z)]
            )
        return late

    def grads_in(t, x, slot):
        gain = gains[1:2, :]

        def total(r):
            grad = ag[slot, pl.ds(r, 32), :].astype(F32)
            value = x[2, pl.ds(r, 32), :] + norm_back(grad, gain, x[0, pl.ds(r, 32), :])
            x[2, pl.ds(r, 32), :] = value
            fl[TL, pl.ds(t * rows + r, 32), :] = value.astype(BF16)

        loop(rows // 32, 32, total)
        grad = dot(fl[TL, pl.ds(t * rows, rows), :], wqo[...].reshape(att, width), NT)
        qd[pl.ds(rows, rows), :] = jnp.where(lane_all >= HEAD_DIM, grad, 0.0).astype(BF16)

    def attend(t, copies, late):
        across, along = copies
        tokens = N_SEQ * rows
        first = []
        for h in range(heads):
            lanes = pl.ds(h * PAIR, PAIR)
            if h < KV_X_FIRST:
                received(along[h])
            else:
                received([across[h]])
            received(late[h])
            kv = kvb[t, h].reshape(tokens, PAIR)
            both = qd[:, lanes]
            scores[...] = dot(kv, both, NT)
            steps = [pl.ds(c * rows, rows) for c in range(N_SEQ)]

            def folded(value, op):
                return op(value.reshape(rows // 8, 8, rows), 0)

            top = folded(scores[steps[0], :rows], jnp.max)
            for here in steps[1:]:
                top = jnp.maximum(top, folded(scores[here, :rows], jnp.max))
            top = jnp.max(top, 0, keepdims=True)
            total = jnp.zeros((8, rows), F32)
            delta = jnp.zeros((8, rows), F32)
            for here in steps:
                weight = jnp.exp(scores[here, :rows] - top)
                scores[here, :rows] = weight
                total = total + folded(weight, jnp.sum)
                delta = delta + folded(weight * scores[here, rows:], jnp.sum)
            scale = 1.0 / jnp.sum(total, 0, keepdims=True)
            delta = jnp.sum(delta, 0, keepdims=True) * scale
            for here in steps:
                probs = scores[here, :rows] * scale
                pd[here, rows:] = probs.astype(BF16)
                pd[here, :rows] = (probs * (scores[here, rows:] - delta)).astype(BF16)
            dks[t, h] = dot(pd[...], both, NN).astype(BF16).reshape(2, N_Z, rows, PAIR)
            if h < DKV_X_FIRST:
                first.append([sender.start(dks.at[t, h, 1], dax.at[t, h], seq_dev(N_Z))])
            else:
                first.append(
                    [
                        sender.start(dks.at[t, h, :, d], dbz.at[t, h - DKV_X_FIRST, d - 1], seq_back(d))
                        for d in range(1, N_Z)
                    ]
                )
            mixed = dot(kv, pd[...], TN).T
            dqf[pl.ds(t * rows, rows), lanes] = jnp.where(lane < HEAD_DIM, mixed[:rows] * 0.125, 0.0).astype(BF16)
            mxf[pl.ds(t * rows, rows), lanes] = jnp.where(lane >= HEAD_DIM, mixed[rows:], 0.0).astype(BF16)
        return first

    def attention_out(t):
        def out(c):
            snd[t, 2, :, pl.ds(c, 256)] = dot(
                mxf[pl.ds(t * rows, rows), :], wqo[:, :, :, pl.ds(c, 256)].reshape(att, 256), NN
            ).astype(BF16)

        loop(width // 256, 256, out)
        return scatter(t, 2)

    def attention_relay(t, first):
        last = []
        for h in range(heads):
            received(first[h])
            if h < DKV_X_FIRST:
                for d in (1, 2, 3, 0):
                    dks[t, h, 0, d] = (
                        dks[t, h, 0, d].astype(F32) + dax[t, h, d].astype(F32)
                    ).astype(BF16)
                    if d > 0:
                        last.append(sender.start(dks.at[t, h, 0, d], daz.at[t, h, d - 1], seq_back(d)))
            else:
                k = h - DKV_X_FIRST
                for side in (1, 0):
                    total = dks[t, h, side, 0].astype(F32)
                    for d in range(N_Z - 1):
                        total = total + dbz[t, k, d, side].astype(F32)
                    dks[t, h, side, 0] = total.astype(BF16)
                last.append(sender.start(dks.at[t, h, 1, 0], dbx.at[t, k], seq_dev(N_Z)))
        return last

    def attention_back(t, last):
        received(last)
        for h in range(heads):
            total = dks[t, h, 0, 0].astype(F32)
            if h < DKV_X_FIRST:
                for d in range(N_Z - 1):
                    total = total + daz[t, h, d].astype(F32)
            else:
                total = total + dbx[t, h - DKV_X_FIRST].astype(F32)
            dkvf[pl.ds(t * rows, rows), pl.ds(h * PAIR, PAIR)] = total.astype(BF16)

        def out(c):
            cols = pl.ds(c, 256)
            snd[t, 3, :, cols] = (
                dot(dkvf[pl.ds(t * rows, rows), :], wkv[:, :, :, cols].reshape(att, 256), NN)
                + dot(dqf[pl.ds(t * rows, rows), :], wqo[:, :, :, cols].reshape(att, 256), NN)
            ).astype(BF16)

        loop(width // 256, 256, out)
        return scatter(t, 3)

    def grad_rows(by_x, by_z):
        index = lax.rem(x_hi + by_x, 2) * N_Z + lax.rem(z + by_z, N_Z)
        return pl.ds(pl.multiple_of(index * chunk, 32), chunk)

    part = chunk // 2

    def part_rows(by_x, by_z, side):
        index = lax.rem(x_hi + by_x, 2) * N_Z + lax.rem(z + by_z, N_Z)
        return index * chunk + side * part

    def add_rows(g, cols, start, count, *terms):
        def add(r):
            here = pl.ds(pl.multiple_of(start + r, 16), 16)
            total = g[here, cols].astype(F32)
            for term in terms:
                total = total + term(pl.ds(r, 16)).astype(F32)
            g[here, cols] = total.astype(BF16)

        loop(count // 16, 16, add)

    def ring_start(g, cols, ks, pass_buf, final):
        def ship(k, d, side, dst, to):
            rows_at = pl.ds(pl.multiple_of(part_rows(k, d, side), 16), part)
            return sender.start(g.at[rows_at, cols], dst, seq_dev(to))

        up = [ship(k, 2, 0, pass_buf.at[0, i], 1) for i, k in enumerate(ks)]
        down = [ship(k, 2, 1, pass_buf.at[1, i], 3) for i, k in enumerate(ks)]
        rest = []
        for i, k in enumerate(ks):
            rest.append(ship(k, 1, 1, final.at[0, i, pl.ds(part, part)], 1))
            rest.append(ship(k, 3, 0, final.at[1, i, pl.ds(0, part)], 3))
        return up, down, rest

    def ring_relay(g, cols, ks, pass_buf, final, copies):
        up, down, rest = copies
        for i, k in enumerate(ks):
            for group, d, side in ((up, 1, 0), (down, 3, 1)):
                received([group[i]])
                start = part_rows(k, d, side)
                add_rows(g, cols, start, part, lambda here, side=side: pass_buf[side, i, here, :])
                rows_at = pl.ds(pl.multiple_of(start, 16), part)
                rest.append(
                    sender.start(g.at[rows_at, cols], final.at[side, i, pl.ds(side * part, part)], seq_dev(d))
                )
        return rest

    class Reduction:
        def __init__(self, g, cut, xa, pa, fa, pb, fb, xb):
            self.g, self.xa, self.pa, self.fa, self.pb, self.fb, self.xb = g, xa, pa, fa, pb, fb, xb
            self.cols_a, self.cols_b = pl.ds(0, cut), pl.ds(cut, g.shape[1] - cut)

        def first(self):
            other = pl.ds(pl.multiple_of((1 - x_hi) * half, 32), half)
            self.across = [sender.start(self.g.at[other, self.cols_a], self.xa, seq_dev(N_Z))]
            self.ring_b = ring_start(self.g, self.cols_b, (1, 0), self.pb, self.fb)

        def second_b(self):
            self.rest_b = ring_relay(self.g, self.cols_b, (1, 0), self.pb, self.fb, self.ring_b)

        def second_a(self):
            received(self.across)
            add_rows(self.g, self.cols_a, x_hi * half, half, lambda here: self.xa[here, :])
            self.ring_a = ring_start(self.g, self.cols_a, (0,), self.pa, self.fa)

        def third(self):
            self.rest_a = ring_relay(self.g, self.cols_a, (0,), self.pa, self.fa, self.ring_a)
            received(self.rest_b)
            for i, k in enumerate((1, 0)):
                add_rows(
                    self.g, self.cols_b, part_rows(k, 0, 0), chunk,
                    lambda here, i=i: self.fb[0, i, here, :], lambda here, i=i: self.fb[1, i, here, :],
                )
                if k == 1:
                    rows_at = pl.ds(pl.multiple_of(part_rows(1, 0, 0), 16), chunk)
                    self.back = [sender.start(self.g.at[rows_at, self.cols_b], self.xb, seq_dev(N_Z))]

        def last(self, store):
            received(self.rest_a)
            received(self.back)
            start = seq * chunk

            def add(r):
                here, out = pl.ds(pl.multiple_of(start + r, 32), 32), pl.ds(r, 32)
                left = self.g[here, self.cols_a].astype(F32)
                for k in range(2):
                    left = left + self.fa[k, 0, out, :].astype(F32)
                right = self.g[here, self.cols_b].astype(F32) + self.xb[out, :].astype(F32)
                store(out, left.astype(BF16), right.astype(BF16))

            loop(chunk // 32, 32, add)

    red_m = Reduction(gmlp, cut_mlp, xa_m, pa_m, fa_m, pb_m, fb_m, xb_m)
    red_a = Reduction(gatt, cut_att, xa_a, pa_a, fa_a, pb_a, fb_a, xb_a)
    red_k = Reduction(gkv, cut_att, xa_k, pa_k, fa_k, pb_k, fb_k, xb_k)

    def store_mlp(here, left, right):
        om[0, here, pl.ds(0, cut_mlp)] = left
        om[0, here, pl.ds(cut_mlp, hid - cut_mlp)] = right

    def joined(left, right, k):
        pieces = []
        for h in range(heads):
            start = h * PAIR + k * HEAD_DIM
            if start < cut_att:
                pieces.append(left[:, start : start + HEAD_DIM])
            else:
                pieces.append(right[:, start - cut_att : start - cut_att + HEAD_DIM])
        return jnp.concatenate(pieces, 1)

    def store_qo(here, left, right):
        oqkv[0, here, :] = joined(left, right, 0)
        oout[here, :] = joined(left, right, 1)

    def store_kv(here, left, right):
        oqkv[1, here, :] = joined(left, right, 0)
        oqkv[2, here, :] = joined(left, right, 1)

    def grads_mlp():
        def tile(c):
            gmlp[pl.ds(c, 256), :] = dot(fl[NU, :, pl.ds(c, 256)], gp[...], TN).astype(BF16)

        loop(width // 256, 256, tile)

    def grads_att():
        def tile(c):
            gatt[pl.ds(c, 256), :] = (
                dot(fl[AL, :, pl.ds(c, 256)], dqf[...], TN) + dot(fl[TL, :, pl.ds(c, 256)], mxf[...], TN)
            ).astype(BF16)

        loop(width // 256, 256, tile)
        red_a.first()

    def grads_kv():
        def tile(c):
            gkv[pl.ds(c, 256), :] = dot(fl[AL, :, pl.ds(c, 256)], dkvf[...], TN).astype(BF16)

        loop(width // 256, 256, tile)
        red_k.first()

    loads[0].wait()
    loads[1].wait()
    mlp_forward(0, xs)
    loads[2].wait()
    mlp_hidden(0)
    loads[3].wait()
    load(7)
    mlp_down(0)
    pl.semaphore_wait(barrier, N_TP - 1 + N_SEQ - 1 + N_TP)
    c_mlp = c_first = scatter(0, 0)
    c_hid = share(hall, 0, HIDDEN_X_FIRST)
    loads[4].wait()
    mlp_back(0, xs)
    slices_out(0, GL, glt, gsl)
    c_mlp = spread(0, summed(0, 0, c_mlp))
    received(c_mlp)
    c_grad = scatter(0, 1)
    for k in range(5, 11):
        loads[k].wait()
    for copy in c_first:
        copy.wait_send()
    c_kv = attention_in(0, xs, 0)
    c_low = sender.start(snd.at[0, 0, mine, :], rx.at[1, mine, :], sec_dev(N_SEC - 1, 0))
    late = pass_along(0, c_kv)
    c_grad = spread(1, summed(0, 1, c_grad))
    late = pass_across(0, c_kv, late)
    c_down = slices_send(0, glt, gsl)
    c_hid = share_rest(hall, 0, HIDDEN_X_FIRST, c_hid)
    received(c_grad)
    grads_in(0, xs, 1)
    c_total = sender.start(
        fl.at[TL, mine, :], rx.at[2, mine, :], sec_dev(N_SEC - 1, 0)
    )
    c_low = section_spread(1, c_low)
    c_dkv = attend(0, c_kv, late)
    c_att = attention_out(0)
    c_dkv = attention_relay(0, c_dkv)
    c_up = send_section(0, xs[0, mine, :] - summed(0, 2, c_att))
    c_down += share_pass(hall, 0, HIDDEN_X_FIRST, c_hid)

    is_last = sec == N_SEC - 1
    loads[11].wait()

    def choose(k):
        def one(r):
            hd[k, pl.ds(r, 32), :] = jnp.where(
                is_last, hd[k, pl.ds(r, 32), :], rx[k, pl.ds(r, 32), :].astype(F32)
            )

        loop(rows // 32, 32, one)

    outs = []

    def emit(k):
        copy = pltpu.make_async_copy(hd.at[k], recon_h.at[k], out_sem.at[k])
        copy.start()
        outs.append(copy)

    def finish(src, dst, k):
        copy = pltpu.make_async_copy(src, dst, out_sem.at[k])
        copy.start()
        outs.append(copy)

    slope = gains[0:1, :]
    c_att = attention_back(0, c_dkv)
    received(c_up)
    choose(0)
    mlp_forward(1, hd)
    mlp_hidden(1)
    mlp_down(1)
    c_mlp = scatter(1, 0)
    c_hid = share_rest(hall, 1, HIDDEN_X_FIRST, share(hall, 1, HIDDEN_X_FIRST))
    grad = summed(0, 3, c_att)
    c_gl = send_section(1, xs[3, mine, :] + norm_back(grad, slope, xs[1, mine, :]))
    c_mlp = spread(2, summed(1, 0, c_mlp))
    received(c_low)
    choose(1)
    received(c_gl)
    choose(3)
    mlp_back(1, hd)
    c_grad = scatter(1, 1)
    received(c_mlp)
    c_kv = attention_in(1, hd, 2)
    emit(1)
    c_total = section_spread(2, c_total)
    grads_mlp()
    c_grad = spread(3, summed(1, 1, c_grad))
    late = pass_along(1, c_kv)
    slices_out(1, GL, glt, gsl)
    late = pass_across(1, c_kv, late)
    red_m.first()
    received(c_total)
    choose(2)
    received(c_grad)
    grads_in(1, hd, 3)
    emit(2)
    c_dkv = attend(1, c_kv, late)
    c_att = attention_out(1)
    red_m.second_b()
    c_down += share_pass(hall, 1, HIDDEN_X_FIRST, c_hid)
    c_dkv = attention_relay(1, c_dkv)
    red_m.second_a()
    grads_att()
    c_up = spread(4, summed(1, 2, c_att))
    c_att = attention_back(1, c_dkv)
    grads_kv()
    c_down += slices_send(1, glt, gsl)
    c_gl = spread(5, summed(1, 3, c_att))
    red_m.third()
    received(c_up)

    def upper(r):
        here = pl.ds(r, 32)
        value = hd[0, here, :]
        pre[here, :] = value - ag[4, here, :].astype(F32)

    loop(rows // 32, 32, upper)
    copy = pltpu.make_async_copy(pre, recon_h.at[0], out_sem.at[0])
    copy.start()
    outs.append(copy)
    red_a.second_b()
    red_a.second_a()
    received(c_gl)

    def lower(r):
        here = pl.ds(r, 32)
        hd[3, here, :] = hd[3, here, :] + norm_back(ag[5, here, :].astype(F32), slope, hd[1, here, :])

    loop(rows // 32, 32, lower)
    emit(3)
    red_k.second_b()
    red_k.second_a()
    red_a.third()
    grads_down(c_down)
    finish(om.at[1], gdn_h, 5)
    red_m.last(store_mlp)
    finish(om.at[0], gup_h, 4)
    red_k.third()
    red_a.last(store_qo)
    finish(oout, gout_h, 7)
    red_k.last(store_kv)
    finish(oqkv, gqkv_h, 6)
    for copy in [c for c in sender.all if all(c is not f for f in c_first)]:
        copy.wait_send()
    for copy in outs:
        copy.wait()


N_COPIES = 320


def per_device(streams, head_streams, gains, w_qkv, w_out, w_up, w_down):
    rows, width = streams.shape[2], streams.shape[3]
    hid = w_up.shape[2]
    local = w_out.shape[2]
    att = 2 * local
    heads = local // HEAD_DIM
    chunk = width // N_SEQ
    half = width // 2
    cut_mlp = 512
    cut_att = 256
    wqkv = jnp.transpose(w_qkv[0], (1, 2, 0)).reshape(3, heads, HEAD_DIM, width)
    wout = jnp.transpose(w_out[0], (1, 0)).reshape(heads, HEAD_DIM, width)
    sizes = (rows, width, hid, att, cut_mlp, cut_att)
    quarter = rows // N_TP
    rest_m, rest_a = hid - cut_mlp, att - cut_att
    n_dx, n_dz = DKV_X_FIRST, heads - DKV_X_FIRST
    vm = pltpu.VMEM

    def ring_buffers(left, right):
        return (
            vm((half, left), BF16), vm((2, 1, chunk // 2, left), BF16), vm((2, 1, chunk, left), BF16),
            vm((2, 2, chunk // 2, right), BF16), vm((2, 2, chunk, right), BF16), vm((chunk, right), BF16),
        )

    scratch = [
        vm((4, rows, width), F32), vm((4, rows, width), F32), vm((2, width), F32),
        vm((heads, 2, HEAD_DIM, width), BF16), vm((heads, 2, HEAD_DIM, width), BF16),
        vm((width, hid), BF16), vm((width, hid), BF16),
        vm((4, rows, width), BF16), vm((2, quarter, width), BF16),
        vm((4, 2 * rows, width), BF16), vm((2 * rows, hid), BF16),
        vm((2, 2, N_Z, rows, hid), BF16), vm((2, width, rows), BF16), vm((chunk, 2 * N_SEQ * rows), BF16),
        vm((2 * rows, att), BF16), vm((2 * rows, att), BF16), vm((2 * rows, att), BF16),
        vm((2, 4, rows, width), BF16), vm((2, 4, N_TP - 1, quarter, width), BF16), vm((6, rows, width), BF16),
        vm((2, heads, 2, N_Z, rows, PAIR), BF16), vm((2, heads, 2, N_Z, rows, PAIR), BF16),
        vm((2, n_dx, N_Z, rows, PAIR), BF16), vm((2, n_dx, N_Z - 1, rows, PAIR), BF16),
        vm((2, n_dz, N_Z - 1, 2, rows, PAIR), BF16), vm((2, n_dz, rows, PAIR), BF16),
        vm((rows, hid), F32), vm((2 * rows, att), BF16),
        vm((N_SEQ * rows, 2 * rows), F32), vm((N_SEQ * rows, 2 * rows), BF16),
        vm((width, hid), BF16), vm((width, att), BF16), vm((width, att), BF16),
        *ring_buffers(cut_mlp, rest_m), *ring_buffers(cut_att, rest_a), *ring_buffers(cut_att, rest_a),
        vm((2, chunk, hid), BF16), vm((3, chunk, local), BF16), vm((chunk, local), BF16),
        pltpu.SemaphoreType.DMA((12,)), pltpu.SemaphoreType.DMA((8,)),
        pltpu.SemaphoreType.DMA((N_COPIES,)), pltpu.SemaphoreType.DMA((N_COPIES,)),
    ]
    any_spec = pl.BlockSpec(memory_space=pl.ANY)
    recon, grad_qkv, grad_out, grad_up, grad_down = pl.pallas_call(
        lambda *refs: kernel(sizes, *refs),
        out_shape=(
            jax.ShapeDtypeStruct((4, rows, width), F32),
            jax.ShapeDtypeStruct((3, chunk, local), BF16),
            jax.ShapeDtypeStruct((chunk, local), BF16),
            jax.ShapeDtypeStruct((chunk, hid), BF16),
            jax.ShapeDtypeStruct((chunk, hid), BF16),
        ),
        in_specs=[any_spec] * 7,
        out_specs=(any_spec,) * 5,
        scratch_shapes=scratch,
        compiler_params=pltpu.CompilerParams(
            collective_id=0, has_side_effects=True, vmem_limit_bytes=67043328
        ),
        name="window",
    )(streams[0], head_streams, gains[0], wqkv, wout, w_up[0], w_down[0])
    grad_qkv = jnp.transpose(grad_qkv, (1, 0, 2))
    return (recon[None], grad_qkv[None], grad_out[None], grad_up[None], grad_down[None])


def solution(mesh):
    return jax.shard_map(
        per_device,
        mesh=mesh,
        in_specs=(
            P("section", None, "seq", None),
            P(None, "seq", None),
            P("section", None, None),
            P("section", None, None, "tp"),
            P("section", None, "tp"),
            P("section", None, "tp"),
            P("section", None, "tp"),
        ),
        out_specs=(
            P("section", None, "seq", None),
            P("section", "seq", None, "tp"),
            P("section", "seq", "tp"),
            P("section", "seq", "tp"),
            P("section", "seq", "tp"),
        ),
        check_vma=False,
    )
```
